32 devices in a mesh: rep: 4 (over x, core), shard: 8 (over z, y).
Axes of the slice: x: 2, y: 2, z: 4, core: 2. Of those that a mesh axis runs over, the one named last changes fastest.
Arguments:
- residual: float32 [4, 1024, 768], P('rep', 'shard'), may hold values from -6 to 6
- segment_ids: int32 [4, 1024], P('rep', 'shard'), may hold values from 0 to 7, never falling along the last dimension, each value on 1 to 256 neighbouring positions
- in_weight: bfloat16 [2, 768, 3352], P(None, 'shard'), may hold values from -0.21875 to 0.21875
- conv_weight: bfloat16 [2, 4, 1792], P(None, None, 'shard'), may hold values from -3 to 3
- conv_bias: bfloat16 [2, 1792], P(None, 'shard'), may hold values from -3 to 3
- a_log: float32 [2, 24], replicated, may hold values from -2 to 2.5
- dt_bias: float32 [2, 24], replicated, may hold values from -7 to -2
- d_skip: float32 [2, 24], replicated, may hold values from 0.5 to 1.5
- norm_gain: bfloat16 [2, 768], P(None, 'shard'), may hold values from 0.5 to 1.5
- gated_gain: bfloat16 [2, 1536], P(None, 'shard'), may hold values from 0.5 to 1.5
- out_weight: bfloat16 [2, 1536, 768], P(None, 'shard'), may hold values from -0.3125 to 0.3125
- out_cotangent: float32 [4, 1024, 768], P('rep', 'shard'), may hold values from -6 to 6
Outputs:
- output: float32 [4, 1024, 768], P('rep', 'shard')
- grad_input: float32 [4, 1024, 768], P('rep', 'shard')
- grad_in_weight: float32 [2, 768, 3352], P(None, 'shard')
- grad_conv_weight: float32 [2, 4, 1792], P(None, None, 'shard')
- grad_conv_bias: float32 [2, 1792], P(None, 'shard')
- grad_a_log: float32 [2, 24], replicated
- grad_dt_bias: float32 [2, 24], replicated
- grad_d_skip: float32 [2, 24], replicated
- grad_norm_gain: float32 [2, 768], P(None, 'shard')
- grad_gated_gain: float32 [2, 1536], P(None, 'shard')
- grad_out_weight: float32 [2, 1536, 768], P(None, 'shard')
The draws below stay inside these ranges and needn't reach their ends.
Inputs may be any that keep to these rules, and one draw needn't show every extreme that they name: `segment_ids`: in each sequence the ids never fall; each document has 1 to 256 tokens and one has exactly 256.
All inputs are finite; a program needn't handle non-finite values.
Results may differ from the reference program's by a relative error of at most 0.011.
Values may be sent and summed in bfloat16 or wider, within the bound.
No kernel may reach another device: no remote copies, remote signals or barrier semaphores. Data moves between devices by JAX's collectives and lax.ppermute only.
A program may use at most 256 MiB of HBM per device.

```python
import math
from functools import partial
import jax
import jax.numpy as jnp
import numpy as np
from jax import lax

D = 768
HEADS = 24
STATE = 128
HEADDIM = 64
CONV = 4
SPAN = 128
LAYERS = 2
INNER = 1536
CONVDIM = 1792
PROJ = 3352
SEQLEN = 1024
SEQS = 4
DOC = 256


def steps_of(key, dims, split, least, high):
    def one(axis_at, parts):
        draws = jax.random.uniform(jax.random.fold_in(jax.random.fold_in(key, 6), axis_at), (parts,), jnp.float32, least / len(split), high / len(split))
        return jnp.repeat(jnp.exp(draws), dims[axis_at] // parts).reshape((-1,) + (1,) * (len(dims) - axis_at - 1))

    loudness = one(*split[0])
    for cut in split[1:]:
        loudness = loudness * one(*cut)
    return loudness


def profile(amount, total, limit, lean):
    loads = [(1 << 20) // math.isqrt(rank ** lean) + 1 for rank in range(2, amount + 1)]
    rest, counts = total - limit - (amount - 1), [1] * (amount - 1)
    while rest > 0:
        movable = [i for i in range(amount - 1) if counts[i] < limit]
        mass, budget = sum([loads[i] for i in movable]), rest
        for i in movable:
            extra = min(limit - counts[i], max(1, budget * loads[i] // mass), rest)
            counts[i] = counts[i] + extra
            rest = rest - extra
    return np.array([limit] + counts)


def ragged_sizes(key, number_of, total, reach, skew):
    if number_of == 2:
        one = jax.random.randint(key, (), max(1, total - reach), min(reach, total - 1) + 1)
        return jnp.stack([one, total - one])
    lengths = jnp.asarray(profile(number_of, total, reach, skew), jnp.int32)
    couples = (number_of - 1) // 2
    giver, taker = lengths[1:1 + 2 * couples:2], lengths[2:2 + 2 * couples:2]
    room = jnp.minimum(giver - 1, reach - taker)
    shifted = jax.random.randint(jax.random.fold_in(key, 1), (couples,), 0, 1 << 20) % (room + 1)
    lengths = lengths.at[1:1 + 2 * couples:2].set(giver - shifted).at[2:2 + 2 * couples:2].set(taker + shifted)
    return lengths[jax.random.permutation(jax.random.fold_in(key, 2), number_of)]


def centred(rng, dims, scale, bound, cuts=(), dtype=jnp.bfloat16):
    values = scale * jax.random.normal(rng, dims, jnp.float32)
    if cuts:
        values = values * steps_of(rng, dims, cuts, -0.22, 0.18)
    return jnp.clip(values, -bound, bound).astype(dtype)


def setup_inputs(seed: int = 0) -> dict:
    streams_of = jax.random.split(jax.random.key(seed), 13)
    residual = centred(streams_of[0], (SEQS, SEQLEN, D), 1.0, 6.0, ((0, 4), (1, 8)), jnp.float32)
    segment_ids = jax.vmap(lambda own: jnp.searchsorted(jnp.cumsum(ragged_sizes(own, 2 * SEQLEN // DOC, SEQLEN, DOC, 0)), jnp.arange(SEQLEN), side="right"))(jax.random.split(streams_of[1], SEQS)).reshape((SEQS, SEQLEN)).astype(jnp.int32)
    in_weight = centred(streams_of[2], (LAYERS, D, PROJ), D ** -0.5, 0.21875, ((1, 8),))
    conv_weight = centred(streams_of[3], (LAYERS, CONV, CONVDIM), CONV ** -0.5, 3.0, ((2, 8),))
    conv_bias = centred(streams_of[4], (LAYERS, CONVDIM), 0.5, 3.0, ((1, 8),))
    a_log = jnp.clip(jax.random.uniform(streams_of[5], (LAYERS, HEADS), jnp.float32, -2.0, 2.5), -2.0, 2.5)
    dt_bias = jnp.clip(jax.random.uniform(streams_of[6], (LAYERS, HEADS), jnp.float32, -7.0, -2.0), -7.0, -2.0)
    d_skip = jnp.clip(jax.random.uniform(streams_of[7], (LAYERS, HEADS), jnp.float32, 0.5, 1.5), 0.5, 1.5)
    norm_gain = jnp.clip(1.0 + 0.1 * jax.random.normal(streams_of[8], (LAYERS, D), jnp.float32), 0.5, 1.5).astype(jnp.bfloat16)
    gated_gain = jnp.clip(1.0 + 0.1 * jax.random.normal(streams_of[9], (LAYERS, INNER), jnp.float32), 0.5, 1.5).astype(jnp.bfloat16)
    out_weight = centred(streams_of[10], (LAYERS, INNER, D), (INNER // 4) ** -0.5, 0.3125, ((1, 8),))
    out_cotangent = centred(streams_of[11], (SEQS, SEQLEN, D), 1.0, 6.0, ((0, 4), (1, 8)), jnp.float32)
    return dict(residual=residual, segment_ids=segment_ids, in_weight=in_weight, conv_weight=conv_weight, conv_bias=conv_bias, a_log=a_log, dt_bias=dt_bias, d_skip=d_skip, norm_gain=norm_gain, gated_gain=gated_gain, out_weight=out_weight, out_cotangent=out_cotangent)


EPS = 1e-05
HIGH = lax.Precision.HIGHEST

def rms(values, gain):
    return values * lax.rsqrt(lax.optimization_barrier(jnp.mean(values * values, axis=-1, keepdims=True)) + EPS) * gain

def span_step(carry, pieces):
    state, last = carry
    xs, bs, cs, dts, das, segs = pieces
    width = segs.shape[0]
    cum = jnp.cumsum(das, axis=0)
    rows = lax.broadcasted_iota(jnp.int32, (width, width), 0)
    cols = lax.broadcasted_iota(jnp.int32, (width, width), 1)
    mask = ((rows >= cols) & (segs[:, None] == segs[None, :])).astype(jnp.float32)
    cum_t = cum.T
    diff = cum_t[:, :, None] - cum_t[:, None, :]
    lmat = jnp.exp(jnp.where(mask[None] > 0, diff, 0.0)) * mask[None]
    scores = jnp.dot(cs, bs.T, precision=HIGH)
    mixing = lmat * scores[None] * dts.T[:, None, :]
    inside = jnp.einsum('hij,jhp->ihp', mixing, xs, precision=HIGH)
    valid = (segs == last).astype(jnp.float32)
    carried = jnp.einsum('in,hnp->ihp', cs, state, precision=HIGH)
    carried = carried * (jnp.exp(cum) * valid[:, None])[:, :, None]
    tail = (segs == segs[-1]).astype(jnp.float32)
    decay = jnp.exp(cum[-1][None, :] - cum) * tail[:, None] * dts
    keep = jnp.exp(cum[-1]) * (segs[-1] == last).astype(jnp.float32)
    fresh = jnp.einsum('jh,jn,jhp->hnp', decay, bs, xs, precision=HIGH)
    return ((state * keep[:, None, None] + fresh, segs[-1]), inside + carried)

def mixer(proj, conv_w, conv_b, dtb, alog, dskip, ggain, seg):
    length = proj.shape[0]
    z_part = proj[:, :INNER]
    xbc = proj[:, INNER:INNER + CONVDIM]
    dt_raw = proj[:, INNER + CONVDIM:]
    padded = jnp.concatenate([jnp.zeros((CONV - 1, CONVDIM), jnp.float32), xbc], 0)
    seg_pad = jnp.concatenate([jnp.full((CONV - 1,), -1, jnp.int32), seg.astype(jnp.int32)])
    total = conv_b
    for k in range(CONV):
        keep = (seg_pad[k:k + length] == seg).astype(jnp.float32)
        total = total + conv_w[k] * padded[k:k + length] * keep[:, None]
    conv_out = jax.nn.silu(total)
    xs = conv_out[:, :INNER].reshape(length, HEADS, HEADDIM)
    bs = conv_out[:, INNER:INNER + STATE]
    cs = conv_out[:, INNER + STATE:]
    dts = jax.nn.softplus(dt_raw + dtb)
    das = -dts * jnp.exp(alog)
    count = length // SPAN
    pieces = (xs.reshape(count, SPAN, HEADS, HEADDIM), bs.reshape(count, SPAN, STATE), cs.reshape(count, SPAN, STATE), dts.reshape(count, SPAN, HEADS), das.reshape(count, SPAN, HEADS), seg.reshape(count, SPAN))
    start = (jnp.zeros((HEADS, STATE, HEADDIM), jnp.float32), jnp.array(-1, jnp.int32))
    _, ys = lax.scan(span_step, start, pieces)
    ys = ys.reshape(length, HEADS, HEADDIM) + dskip[None, :, None] * xs
    gated = ys.reshape(length, INNER) * jax.nn.silu(z_part)
    return rms(gated, ggain)

def one_sequence(totals, pieces):
    u_now, seg, cot = pieces
    in_weight, conv_weight, conv_bias, a_log, dt_bias, d_skip, norm_gain, gated_gain, out_weight = totals[1]
    saved = []
    for layer in range(LAYERS):
        normed, norm_pull = jax.vjp(rms, u_now, norm_gain[layer].astype(jnp.float32))
        hidden = normed.astype(jnp.bfloat16)
        proj = jnp.dot(hidden, in_weight[layer], preferred_element_type=jnp.float32)
        yn, mix_pull = jax.vjp(partial(mixer, seg=seg), proj, conv_weight[layer].astype(jnp.float32), conv_bias[layer].astype(jnp.float32), dt_bias[layer], a_log[layer], d_skip[layer], gated_gain[layer].astype(jnp.float32))
        yn_b = yn.astype(jnp.bfloat16)
        u_now = u_now + jnp.dot(yn_b, out_weight[layer], preferred_element_type=jnp.float32)
        saved.append((hidden, norm_pull, mix_pull, yn_b))
    grad = cot
    sums = list(totals[0])
    for layer in reversed(range(LAYERS)):
        hidden, norm_pull, mix_pull, yn_b = saved[layer]
        grad_b = grad.astype(jnp.bfloat16)
        g_out = jnp.dot(yn_b.T, grad_b, preferred_element_type=jnp.float32)
        d_yn = jnp.dot(grad_b, out_weight[layer].T, preferred_element_type=jnp.float32)
        d_proj, g_cw, g_cb, g_dtb, g_alog, g_dsk, g_gg = mix_pull(d_yn)
        d_proj_b = d_proj.astype(jnp.bfloat16)
        g_in = jnp.dot(hidden.T, d_proj_b, preferred_element_type=jnp.float32)
        d_h = jnp.dot(d_proj_b, in_weight[layer].T, preferred_element_type=jnp.float32)
        d_u, g_ng = norm_pull(d_h)
        grad = grad + d_u
        layer_terms = (g_in, g_cw, g_cb, g_alog, g_dtb, g_dsk, g_ng, g_gg, g_out)
        for index in range(9):
            sums[index] = sums[index].at[layer].add(layer_terms[index])
    return ((tuple(sums), totals[1]), (u_now, grad))

def reference(residual, segment_ids, in_weight, conv_weight, conv_bias, a_log, dt_bias, d_skip, norm_gain, gated_gain, out_weight, out_cotangent):
    params = (in_weight, conv_weight, conv_bias, a_log, dt_bias, d_skip, norm_gain, gated_gain, out_weight)
    zeros = tuple((jnp.zeros(p.shape, jnp.float32) for p in params))
    (sums, _), (outputs, grads) = lax.scan(one_sequence, (zeros, params), (residual, segment_ids, out_cotangent))
    return (outputs, grads, sums[0], sums[1], sums[2], sums[3], sums[4], sums[5], sums[6], sums[7], sums[8])
```

```python
from functools import partial

import jax
import jax.numpy as jnp
from jax import lax
from jax.experimental import pallas as pl
from jax.experimental.pallas import tpu as pltpu
from jax.sharding import Mesh
from jax.sharding import PartitionSpec as P

HEADS = 24
STATE = 128
HEADDIM = 64
CONV = 4
SPAN = 128
INNER = 1536
CONVDIM = 1792


EPS = 1e-05
HIGH = lax.Precision.HIGHEST


def passed_along(x, axis, by):
    count = lax.axis_size(axis)
    pairs = [(i, i + by) for i in range(count) if 0 <= i + by < count]
    return lax.ppermute(x, axis, pairs)


def carried_in(part, axis, combine, identity, reverse):
    count = lax.axis_size(axis)
    place = lax.axis_index(axis)
    ahead = count - 1 - place if reverse else place
    gathered = jax.tree.map(lambda a: lax.all_gather(a, axis), part)
    state = jax.tree.map(lambda a, e: jnp.zeros_like(a) + jnp.asarray(e, a.dtype), part, identity)

    def one(turn, state):
        source = count - 1 - turn if reverse else turn
        return combine(
            state, jax.tree.map(lambda a: lax.dynamic_index_in_dim(a, source, 0, False), gathered)
        )

    return lax.fori_loop(0, ahead, one, state)


def rms(values, gain):
    return values * lax.rsqrt(jnp.mean(values * values, axis=-1, keepdims=True) + EPS) * gain


def span_step(carry, pieces):
    state, last = carry
    xs, bs, cs, dts, das, segs = pieces
    width = segs.shape[0]
    cum = jnp.cumsum(das, axis=0)
    rows = lax.broadcasted_iota(jnp.int32, (width, width), 0)
    cols = lax.broadcasted_iota(jnp.int32, (width, width), 1)
    mask = ((rows >= cols) & (segs[:, None] == segs[None, :])).astype(jnp.float32)
    cum_t = cum.T
    diff = cum_t[:, :, None] - cum_t[:, None, :]
    lmat = jnp.exp(jnp.where(mask[None] > 0, diff, 0.0)) * mask[None]
    scores = jnp.dot(cs, bs.T, precision=HIGH)
    mixing = lmat * scores[None] * dts.T[:, None, :]
    inside = jnp.einsum("hij,jhp->ihp", mixing, xs, precision=HIGH)
    valid = (segs == last).astype(jnp.float32)
    carried = jnp.einsum("in,hnp->ihp", cs, state, precision=HIGH)
    carried = carried * (jnp.exp(cum) * valid[:, None])[:, :, None]
    tail = (segs == segs[-1]).astype(jnp.float32)
    decay = jnp.exp(cum[-1][None, :] - cum) * tail[:, None] * dts
    keep = jnp.exp(cum[-1]) * (segs[-1] == last).astype(jnp.float32)
    fresh = jnp.einsum("jh,jn,jhp->hnp", decay, bs, xs, precision=HIGH)
    return ((state * keep[:, None, None] + fresh, segs[-1]), inside + carried)


def front(xbc, rim, dt_raw, conv_w, conv_b, dtb, alog, keeps):
    length = xbc.shape[0]
    padded = jnp.concatenate([rim, xbc], 0)
    total = conv_b
    for k in range(CONV):
        total = total + conv_w[k] * padded[k : k + length] * keeps[k][:, None]
    conv_out = jax.nn.silu(total)
    xs = conv_out[:, :INNER].reshape(length, HEADS, HEADDIM)
    bs = conv_out[:, INNER : INNER + STATE]
    cs = conv_out[:, INNER + STATE :]
    dts = jax.nn.softplus(dt_raw + dtb)
    return (xs, bs, cs, dts, -dts * jnp.exp(alog))


def local_states(xs, bs, cs, dts, das, seg, seg_prev):
    length = seg.shape[0]
    count = length // SPAN
    pieces = (
        xs.reshape(count, SPAN, HEADS, HEADDIM),
        bs.reshape(count, SPAN, STATE),
        cs.reshape(count, SPAN, STATE),
        dts.reshape(count, SPAN, HEADS),
        das.reshape(count, SPAN, HEADS),
        seg.reshape(count, SPAN),
    )
    start = (jnp.zeros((HEADS, STATE, HEADDIM), jnp.float32), seg[0])
    (final, _), ys = lax.scan(span_step, start, pieces)
    passing = jnp.exp(jnp.sum(das, axis=0)) * (seg[-1] == seg_prev).astype(jnp.float32)
    return (ys.reshape(length, HEADS, HEADDIM), passing, final)


def finish(z_part, xs, cs, das, y_local, entering, dskip, ggain, seg, seg_prev):
    length = seg.shape[0]
    cum = jnp.cumsum(das, axis=0)
    valid = (seg == seg_prev).astype(jnp.float32)
    from_before = jnp.einsum("tn,hnp->thp", cs, entering, precision=HIGH)
    from_before = from_before * (jnp.exp(cum) * valid[:, None])[:, :, None]
    ys = y_local + from_before + dskip[None, :, None] * xs
    gated = ys.reshape(length, INNER) * jax.nn.silu(z_part)
    return rms(gated, ggain)


def combine(earlier, later):
    return (earlier[0] * later[0], later[0][:, None, None] * earlier[1] + later[1])


def gather_layer(
    in_weight, out_weight, conv_weight, conv_bias, norm_gain, gated_gain, layer, again
):
    if again:
        return (
            lax.all_gather(in_weight[layer], "shard", axis=0, tiled=True),
            lax.all_gather(out_weight[layer], "shard", axis=0, tiled=True),
            lax.all_gather(conv_weight[layer], "shard", axis=1, tiled=True),
            lax.all_gather(conv_bias[layer], "shard", axis=0, tiled=True),
            lax.all_gather(norm_gain[layer], "shard", axis=0, tiled=True),
            lax.all_gather(gated_gain[layer], "shard", axis=0, tiled=True),
        )
    return (
        lax.all_gather(in_weight[layer], "shard", axis=0, tiled=True),
        lax.all_gather(out_weight[layer], "shard", axis=0, tiled=True),
        lax.all_gather(conv_weight[layer], "shard", axis=1, tiled=True),
        lax.all_gather(conv_bias[layer], "shard", axis=0, tiled=True),
        lax.all_gather(norm_gain[layer], "shard", axis=0, tiled=True),
        lax.all_gather(gated_gain[layer], "shard", axis=0, tiled=True),
    )


def per_device(
    residual,
    segment_ids,
    in_weight,
    conv_weight,
    conv_bias,
    a_log,
    dt_bias,
    d_skip,
    norm_gain,
    gated_gain,
    out_weight,
    out_cotangent,
):
    u_now = residual[0]
    seg = segment_ids[0]
    length = seg.shape[0]
    layers = in_weight.shape[0]
    rim_ids = passed_along(seg[length - CONV + 1 :], "shard", 1)
    seg_ext = jnp.concatenate([rim_ids, seg])
    seg_prev = rim_ids[CONV - 2]
    keeps = jnp.stack([(seg_ext[k : k + length] == seg).astype(jnp.float32) for k in range(CONV)])
    identity = (jnp.ones((HEADS,), jnp.float32), jnp.zeros((HEADS, STATE, HEADDIM), jnp.float32))
    saved = []
    for layer in range(layers):
        weights = gather_layer(
            in_weight, out_weight, conv_weight, conv_bias, norm_gain, gated_gain, layer, False
        )
        w_in, w_out, conv_w, conv_b, n_gain, g_gain = weights
        normed, norm_pull = jax.vjp(rms, u_now, n_gain.astype(jnp.float32))
        hidden = normed.astype(jnp.bfloat16)
        proj = jnp.dot(hidden, w_in, preferred_element_type=jnp.float32)
        z_part = proj[:, :INNER]
        xbc = proj[:, INNER : INNER + CONVDIM]
        dt_raw = proj[:, INNER + CONVDIM :]
        rim = passed_along(xbc[length - CONV + 1 :], "shard", 1)
        feats, front_pull = jax.vjp(
            partial(front, keeps=keeps),
            xbc,
            rim,
            dt_raw,
            conv_w.astype(jnp.float32),
            conv_b.astype(jnp.float32),
            dt_bias[layer],
            a_log[layer],
        )
        xs, bs, cs, dts, das = feats
        (y_local, passing, final), local_pull = jax.vjp(
            partial(local_states, seg=seg, seg_prev=seg_prev), xs, bs, cs, dts, das
        )
        entering = carried_in((passing, final), "shard", combine, identity, False)[1]
        yn, finish_pull = jax.vjp(
            partial(finish, seg=seg, seg_prev=seg_prev),
            z_part,
            xs,
            cs,
            das,
            y_local,
            entering,
            d_skip[layer],
            g_gain.astype(jnp.float32),
        )
        yn_b = yn.astype(jnp.bfloat16)
        u_now = u_now + jnp.dot(yn_b, w_out, preferred_element_type=jnp.float32)
        kept = None
        saved.append(
            (hidden, norm_pull, front_pull, local_pull, finish_pull, passing, entering, yn_b, kept)
        )
    grad = out_cotangent[0]
    owned = [None] * layers
    heads = [None] * layers
    for layer in reversed(range(layers)):
        hidden, norm_pull, front_pull, local_pull, finish_pull, passing, entering, yn_b, kept = (
            saved[layer]
        )
        weights = gather_layer(
            in_weight, out_weight, conv_weight, conv_bias, norm_gain, gated_gain, layer, True
        )
        w_in, w_out = (weights[0], weights[1])
        grad_b = grad.astype(jnp.bfloat16)
        g_out = jnp.dot(yn_b.T, grad_b, preferred_element_type=jnp.float32)
        d_yn = jnp.dot(grad_b, w_out.T, preferred_element_type=jnp.float32)
        d_z, d_xs1, d_cs1, d_das1, d_local, d_enter, g_dsk, g_gg = finish_pull(d_yn)
        later = carried_in((passing, d_enter), "shard", combine, identity, True)[1]
        d_passing = jnp.sum(later * entering, axis=(1, 2))
        d_xs2, d_bs, d_cs2, d_dts, d_das2 = local_pull((d_local, d_passing, later))
        d_xbc, d_rim, d_dtr, g_cw, g_cb, g_dtb, g_alog = front_pull(
            (d_xs1 + d_xs2, d_bs, d_cs1 + d_cs2, d_dts, d_das1 + d_das2)
        )
        back_rim = passed_along(d_rim, "shard", -1)
        d_xbc = d_xbc.at[length - CONV + 1 :].add(back_rim)
        d_proj = jnp.concatenate([d_z, d_xbc, d_dtr], 1).astype(jnp.bfloat16)
        g_in = jnp.dot(hidden.T, d_proj, preferred_element_type=jnp.float32)
        d_h = jnp.dot(d_proj, w_in.T, preferred_element_type=jnp.float32)
        d_u, g_ng = norm_pull(d_h)
        grad = grad + d_u
        shares = (
            lax.psum_scatter(g_in, "shard", scatter_dimension=0, tiled=True),
            lax.psum_scatter(g_out, "shard", scatter_dimension=0, tiled=True),
            lax.psum_scatter(g_cw, "shard", scatter_dimension=1, tiled=True),
            lax.psum_scatter(g_cb, "shard", scatter_dimension=0, tiled=True),
            lax.psum_scatter(g_ng, "shard", scatter_dimension=0, tiled=True),
            lax.psum_scatter(g_gg, "shard", scatter_dimension=0, tiled=True),
        )
        shares = lax.psum((shares[0], shares[1], shares[2], shares[3], shares[4], shares[5]), "rep")
        owned[layer] = shares
        heads[layer] = jnp.stack([g_alog, g_dtb, g_dsk])
    grads_in = jnp.stack([owned[k][0] for k in range(layers)])
    grads_out = jnp.stack([owned[k][1] for k in range(layers)])
    grads_cw = jnp.stack([owned[k][2] for k in range(layers)])
    grads_cb = jnp.stack([owned[k][3] for k in range(layers)])
    grads_ng = jnp.stack([owned[k][4] for k in range(layers)])
    grads_gg = jnp.stack([owned[k][5] for k in range(layers)])
    head_sums = lax.psum(jnp.stack(heads), ("rep", "shard"))
    return (
        u_now[None],
        grad[None],
        grads_in,
        grads_cw,
        grads_cb,
        head_sums[:, 0],
        head_sums[:, 1],
        head_sums[:, 2],
        grads_ng,
        grads_gg,
        grads_out,
    )


AXES = ("x", "c", "zh", "zl", "y")
LANES = 128
ROWS = 16
WIDE = 2 * LANES
COLS = 6 * LANES
VMEM_LIMIT = 56 * 1024 * 1024
BF = jnp.bfloat16
F32 = jnp.float32


def nn(a, b, precision=None):
    return lax.dot_general(
        a, b, (((1,), (0,)), ((), ())), precision=precision, preferred_element_type=F32
    )


def nt(a, b, precision=None):
    return lax.dot_general(
        a, b, (((1,), (1,)), ((), ())), precision=precision, preferred_element_type=F32
    )


def tn(a, b, precision=None):
    return lax.dot_general(
        a, b, (((0,), (0,)), ((), ())), precision=precision, preferred_element_type=F32
    )


def sigmoid(v):
    return 1.0 / (1.0 + jnp.exp(-v))


def softplus(v):
    return jnp.maximum(v, 0.0) + jnp.log1p(jnp.exp(-jnp.abs(v)))


def iota(shape, axis):
    return lax.broadcasted_iota(jnp.int32, shape, axis)


class Heads:
    def __init__(self, heads, p):
        self.heads = heads
        self.p = p
        self.base = heads * p - LANES

    def spread(self, v):
        lane = iota((v.shape[0], WIDE), 1)
        out = jnp.zeros((v.shape[0], WIDE), F32)
        for h in range(self.heads):
            col = v[:, self.base + h : self.base + h + 1]
            inside = (lane >= h * self.p) & (lane < (h + 1) * self.p)
            out = jnp.where(inside, col, out)
        return out

    def gather_matrix(self):
        row = iota((WIDE, LANES), 0)
        lane = iota((WIDE, LANES), 1)
        hit = jnp.zeros((WIDE, LANES), F32)
        for h in range(self.heads):
            inside = (row >= h * self.p) & (row < (h + 1) * self.p) & (lane == self.base + h)
            hit = jnp.where(inside, 1.0, hit)
        return hit

    def gather(self, v):
        return nn(v, self.gather_matrix(), HIGH)

    def masked(self, v):
        lane = iota(v.shape, 1)
        return [
            jnp.where((lane >= h * self.p) & (lane < (h + 1) * self.p), v, 0.0)
            for h in range(self.heads)
        ]

    def valid(self, rows):
        lane = iota((rows, LANES), 1)
        return (lane >= self.base) & (lane < self.base + self.heads)


def column(row, span):
    return jnp.transpose(jnp.broadcast_to(row, (span, row.shape[1])))


def fill_ids(seg_ref, ids, count, span):
    ids[...] = jnp.full(ids.shape, -1.0, F32)

    def one(k, _):
        row = seg_ref[k][0:1, :]
        ids[pl.ds(pl.multiple_of(8 + k * span, 8), span), :] = column(row, span)
        return 0

    lax.fori_loop(0, count, one, 0)


def times4(mask):
    return jnp.concatenate([mask] * 4, axis=1)


def taps_in(xpad, ids, start, cols, cw, span):
    near = xpad[pl.ds(start, span + 8), :]
    near_ids = ids[pl.ds(start, span + 8), :]
    total = cw[4:5, :] + cw[3:4, :] * near[8:]
    kept = []
    for k in range(3):
        same = times4((near_ids[5 + k : 5 + k + span] == cols).astype(F32))
        kept.append(near[5 + k : 5 + k + span] * same)
        total = total + cw[k : k + 1, :] * kept[k]
    kept.append(near[8:])
    return total, kept


def span_terms(heads, zdt, hp, seg_ref, k, span):
    row = seg_ref[k][0:1, :]
    before = seg_ref[jnp.maximum(k - 1, 0)][0:1, span - 1 : span]
    last = row[:, span - 1 : span]
    cols = column(row, span)
    raw = zdt[:, LANES:] + hp[0:1, :LANES]
    ok = heads.valid(span)
    dts = jnp.where(ok, softplus(raw), 0.0)
    rate = jnp.exp(hp[1:2, :LANES])
    das = -dts * rate
    ri, ci = iota((span, span), 0), iota((span, span), 1)
    tri = (ri >= ci).astype(F32)
    cum = nn(tri, das, HIGH)
    mask = (ri >= ci) & (cols == row)
    total = cum[span - 1 : span, :]
    enter = jnp.exp(cum) * (cols == before).astype(F32)
    leave = jnp.exp(total - cum) * (cols == last).astype(F32)
    keep = jnp.exp(total) * (last == before).astype(F32)
    cum_t = jnp.transpose(cum)
    decays = []
    for h in range(heads.heads):
        at = heads.base + h
        diff = cum[:, at : at + 1] - cum_t[at : at + 1, :]
        decays.append(jnp.where(mask, jnp.exp(jnp.where(mask, diff, 0.0)), 0.0))
    return raw, dts, rate, das, enter, leave, keep, decays, cols


def forward_kernel(heads, count, span, with_back, *refs):
    if with_back:
        h_ref, w_ref, wo_ref, cw_ref, hp_ref, seg_ref, gb_ref = refs[:7]
        refs = refs[7:]
    else:
        h_ref, w_ref, wo_ref, cw_ref, hp_ref, seg_ref = refs[:6]
        refs = refs[6:]
    out_ref, stat_ref, zdt_ref, xbc_ref, y_ref, s_ref, ids, state = refs
    fill_ids(seg_ref, ids, count, span)
    state[...] = jnp.zeros_like(state)
    xbc_ref[pl.ds(0, 8), :] = jnp.zeros((8, xbc_ref.shape[1]), F32)
    cw = cw_ref[...]
    hp = hp_ref[...]

    def one(k, _):
        start = pl.multiple_of(k * span, span)
        proj = nn(h_ref[k][:span, :], w_ref[...])
        zdt = proj[:, :WIDE]
        zdt_ref[pl.ds(start, span), :] = zdt
        xbc_ref[pl.ds(start + 8, span), :] = proj[:, WIDE:]
        raw, dts, rate, das, enter, leave, keep, decays, cols = span_terms(
            heads, zdt, hp, seg_ref, k, span
        )
        pre, kept = taps_in(xbc_ref, ids, start, cols, cw, span)
        xc = pre * sigmoid(pre)
        x = xc[:, :WIDE]
        b16 = xc[:, WIDE : WIDE + LANES].astype(BF)
        c16 = xc[:, WIDE + LANES :].astype(BF)
        scores = nt(c16, b16)
        mixing = jnp.concatenate([(d * scores).astype(BF) for d in decays], axis=1)
        xdt = x * heads.spread(dts)
        stacked = jnp.concatenate([v.astype(BF) for v in heads.masked(xdt)], axis=0)
        y = nn(mixing, stacked)
        s_now = state[...]
        s_ref[k] = s_now
        y = y + nn(c16, s_now.astype(BF)) * heads.spread(enter)
        y = y + x * hp[2:3, :]
        fresh = tn(b16, (x * heads.spread(leave * dts)).astype(BF))
        state[...] = s_now * heads.spread(keep) + fresh
        y_ref[pl.ds(start, span), :] = y
        z = zdt
        gated = y * (z * sigmoid(z))
        ones = jnp.ones((8, WIDE), F32)
        squares = nt(ones, gated * gated, HIGH)
        scaled = gated * hp[3:4, :]
        out_ref[k, pl.ds(0, span), :] = nn(scaled.astype(BF), wo_ref[...]).astype(BF)
        if with_back:
            d_yn = nt(gb_ref[k][:span, :], wo_ref[...])
            dots = nt(ones, scaled * d_yn, HIGH)
            pick = iota((8, LANES), 0) == 0
            stat_ref[k] = jnp.where(pick, squares, dots)
        else:
            stat_ref[k] = squares
            tail = jnp.concatenate(
                [squares, squares], axis=0
            )
            rest = jnp.zeros((ROWS, COLS - LANES), F32)
            out_ref[k, pl.ds(span, ROWS), :] = jnp.concatenate([tail, rest], axis=1).astype(BF)
        return 0

    lax.fori_loop(0, count, one, 0)


def backward_kernel(heads, count, span, *refs):
    (gb_ref, w_ref, wo_ref, cw_ref, hp_ref, seg_ref, rq_ref, zdt_ref, xbc_ref, y_ref, s_ref) = refs[:11]
    dproj_ref, dh_ref, yn_ref, sm_ref, ids, dpad, d_state = refs[11:]
    fill_ids(seg_ref, ids, count, span)
    d_state[...] = jnp.zeros_like(d_state)
    sm_ref[...] = jnp.zeros_like(sm_ref)
    length = count * span
    dpad[pl.ds(length, 8), :] = jnp.zeros((8, dpad.shape[1]), F32)
    cw = cw_ref[...]
    hp = hp_ref[...]
    gain = hp[3:4, :]

    def add(row, value):
        sm_ref[row : row + 1, : value.shape[1]] += value

    def one(turn, _):
        k = count - 1 - turn
        start = pl.multiple_of(k * span, span)
        zdt = zdt_ref[pl.ds(start, span), :]
        raw, dts, rate, das, enter, leave, keep, decays, cols = span_terms(
            heads, zdt, hp, seg_ref, k, span
        )
        pre, kept = taps_in(xbc_ref, ids, start, cols, cw, span)
        sp = sigmoid(pre)
        xc = pre * sp
        x = xc[:, :WIDE]
        b16 = xc[:, WIDE : WIDE + LANES].astype(BF)
        c16 = xc[:, WIDE + LANES :].astype(BF)
        y = y_ref[pl.ds(start, span), :]
        z = zdt
        sz = sigmoid(z)
        silu = z * sz
        gated = y * silu
        rq = rq_ref[k]
        r = jnp.concatenate([column(rq[0:1, :], span)] * 2, axis=1)
        q = jnp.concatenate([column(rq[1:2, :], span)] * 2, axis=1)
        normed = gated * r
        yn_ref[pl.ds(start, span), :] = (normed * gain).astype(BF)
        d_yn = nt(gb_ref[k][:span, :], wo_ref[...])
        add(5, jnp.sum(normed * d_yn, axis=0, keepdims=True))
        d_gated = r * gain * d_yn - gated * q
        dy = d_gated * silu
        dz = d_gated * y * (sz * (1.0 + z * (1.0 - sz)))
        add(6, jnp.sum(dy * x, axis=0, keepdims=True))
        dx = hp[2:3, :] * dy
        s_now = s_ref[k]
        s16 = s_now.astype(BF)
        dy_in = dy * heads.spread(enter)
        dy_in16 = dy_in.astype(BF)
        from_state = nn(c16, s16)
        d_cum = heads.gather(dy_in * from_state)
        dc = nt(dy_in16, s16)
        ds_next = d_state[...]
        ds16 = ds_next.astype(BF)
        wide_leave = heads.spread(leave * dts)
        b_ds = nn(b16, ds16)
        dx = dx + b_ds * wide_leave
        db = nt((x * wide_leave).astype(BF), ds16)
        d_leave = heads.gather(x * b_ds)
        through = d_leave * leave * dts
        held = jnp.sum(ds_next * s_now, axis=0, keepdims=True)
        held = heads.gather(jnp.broadcast_to(held, (8, WIDE)))[0:1, :] * keep
        d_state[...] = ds_next * heads.spread(keep) + tn(c16, dy_in16)
        scores = nt(c16, b16)
        wide_dt = heads.spread(dts)
        xdt = x * wide_dt
        dys = jnp.concatenate([v.astype(BF) for v in heads.masked(dy)], axis=0)
        d_mix = nt(dys, xdt.astype(BF))
        d_scores = jnp.zeros((span, span), F32)
        mixings = []
        lane = iota((span, LANES), 1)
        line = iota((LANES, span), 0)
        firsts = jnp.zeros((span, LANES), F32)
        seconds = jnp.zeros((LANES, span), F32)
        for h in range(heads.heads):
            dm = d_mix[h * span : (h + 1) * span, :] * decays[h]
            d_scores = d_scores + dm
            mixings.append((decays[h] * scores).astype(BF))
            flow = dm * scores
            at = heads.base + h
            firsts = jnp.where(lane == at, jnp.sum(flow, axis=1, keepdims=True), firsts)
            seconds = jnp.where(line == at, jnp.sum(flow, axis=0, keepdims=True), seconds)
        d_cum = d_cum + firsts - jnp.transpose(seconds) - through
        d_xdt = tn(jnp.concatenate(mixings, axis=0), dys)
        ds_16 = d_scores.astype(BF)
        dc = dc + nn(ds_16, b16)
        db = db + tn(ds_16, c16)
        dx = dx + d_xdt * wide_dt
        d_dt = heads.gather(x * d_xdt) + d_leave * leave
        at_end = held + jnp.sum(through, axis=0, keepdims=True)
        ri, ci = iota((span, span), 0), iota((span, span), 1)
        d_das = nn((ri <= ci).astype(F32), d_cum, HIGH) + at_end
        d_dt = d_dt - d_das * rate
        add(7, jnp.sum(d_das * das, axis=0, keepdims=True))
        d_raw = jnp.where(heads.valid(span), d_dt * sigmoid(raw), 0.0)
        add(8, jnp.sum(d_raw, axis=0, keepdims=True))
        dzdt = dz + jnp.concatenate([jnp.zeros((span, LANES), F32), d_raw], axis=1)
        d_pre = jnp.concatenate([dx, db, dc], axis=1) * (sp * (1.0 + pre * (1.0 - sp)))
        dpad[pl.ds(start, span), :] = d_pre
        add(4, jnp.sum(d_pre, axis=0, keepdims=True))
        for t in range(4):
            add(t, jnp.sum(d_pre * kept[t], axis=0, keepdims=True))
        d_xbc = cw[3:4, :] * d_pre
        near = dpad[pl.ds(start, span + 8), :]
        near_ids = ids[pl.ds(start + 8, span + 8), :]
        for t in range(3):
            ahead = 3 - t
            same = times4((near_ids[ahead : ahead + span] == cols).astype(F32))
            d_xbc = d_xbc + cw[t : t + 1, :] * near[ahead : ahead + span] * same
        d_proj = jnp.concatenate([dzdt, d_xbc], axis=1).astype(BF)
        dproj_ref[pl.ds(start, span), :] = d_proj
        dh_ref[k] = nt(d_proj, w_ref[...]).astype(BF)
        return 0

    lax.fori_loop(0, count, one, 0)


def call(kernel, outs, scratch, *args):
    whole = pl.BlockSpec(memory_space=pltpu.VMEM)
    return pl.pallas_call(
        kernel,
        out_shape=[jax.ShapeDtypeStruct(s, d) for s, d in outs],
        in_specs=[whole] * len(args),
        out_specs=[whole] * len(outs),
        scratch_shapes=scratch,
        compiler_params=pltpu.CompilerParams(vmem_limit_bytes=VMEM_LIMIT),
    )(*args)


def swap(x, axes, by):
    count = lax.axis_size(axes)
    return lax.ppermute(x, axes, [(i, i ^ by) for i in range(count)])


def to_plane(x):
    pairs = []
    for i in range(16):
        xx, cc, zh, zl = (i >> 3) & 1, (i >> 2) & 1, (i >> 1) & 1, i & 1
        pairs.append((i, (zl << 3) | (zh << 2) | (cc << 1) | xx))
    return lax.ppermute(x, ("x", "c", "zh", "zl"), pairs)


def in_order(parts, me, order):
    stacked = jnp.stack(parts)
    return jnp.concatenate([lax.dynamic_index_in_dim(stacked, me ^ j, 0, True) for j in order])


def gather4(x, axes, order=(0, 1, 2, 3)):
    me = lax.axis_index(axes)
    return in_order([x] + [swap(x, axes, k) for k in (1, 2, 3)], me, order)


def gather_plane(x):
    quad = gather4(x, ("x", "y"))
    other = swap(quad, "c", 1)
    first = lax.axis_index("c") == 0
    return jnp.concatenate([jnp.where(first, quad, other), jnp.where(first, other, quad)])


def scatter_plane(x):
    halves = x.reshape((2, 4) + x.shape[1:])
    c = lax.axis_index("c")
    mine = lax.dynamic_index_in_dim(halves, c, 0, False)
    theirs = swap(lax.dynamic_index_in_dim(halves, 1 - c, 0, False), "c", 1)
    half = (mine.astype(F32) + theirs.astype(F32)).astype(BF)
    me = lax.axis_index(("x", "y"))
    total = lax.dynamic_index_in_dim(half, me, 0, False).astype(F32)
    for k in (1, 2, 3):
        got = swap(lax.dynamic_index_in_dim(half, me ^ k, 0, False), ("x", "y"), k)
        total = total + got.astype(F32)
    return total


def sum_plane(x):
    total = x
    for k in (1, 2, 3):
        total = total + swap(x, ("x", "y"), k)
    return total + swap(total, "c", 1)


def split16(v):
    high = v.astype(BF)
    return high, (v - high.astype(F32)).astype(BF)


def plane_device(
    residual,
    segment_ids,
    in_weight,
    conv_weight,
    conv_bias,
    a_log,
    dt_bias,
    d_skip,
    norm_gain,
    gated_gain,
    out_weight,
    out_cotangent,
):
    span = residual.shape[1]
    width = residual.shape[2]
    layers = in_weight.shape[0]
    rows = in_weight.shape[1]
    group = 8
    heads = Heads(HEADS // group, HEADDIM)
    chan = heads.heads * heads.p
    x_i, c_i, y_i = lax.axis_index("x"), lax.axis_index("c"), lax.axis_index("y")
    z_i = lax.axis_index(("zh", "zl"))
    rank = 4 * c_i + 2 * x_i + y_i

    per = conv_bias.shape[1]
    narrow = lambda v: jnp.pad(v, ((0, 0), (0, WIDE - v.shape[1])))
    small = jnp.concatenate(
        [narrow(conv_weight.reshape(layers * CONV, per)), narrow(conv_bias), narrow(norm_gain)]
    )
    small = jnp.pad(small, ((0, -small.shape[0] % ROWS), (0, 0)))
    pair = swap(small, "y", 1)
    pair = jnp.stack([jnp.where(y_i == 0, small, pair), jnp.where(y_i == 0, pair, small)])
    small = gather4(pair, ("zh", "zl")).reshape((group,) + small.shape).astype(F32)
    lay = lambda at, size: small[:, at, :size].reshape(-1)
    n_gain = [lay(layers * (CONV + 1) + layer, rows) for layer in range(layers)]

    u_mine = residual[0]
    ids_row = jnp.broadcast_to(segment_ids[0].astype(BF)[None, :], (ROWS, span))
    first = jnp.concatenate(
        [
            rms(u_mine, n_gain[0]).astype(BF),
            jnp.pad(ids_row, ((0, 0), (0, width - span))),
        ]
    )
    first = to_plane(first)
    hx = gather_plane(first)
    seg = hx[:, span : span + 8, :span].astype(F32)

    def columns(layer, which):
        w = in_weight[layer]
        pick = lambda at, size: lax.dynamic_slice_in_dim(w, at, size, 1)
        zeros = lambda n: jnp.zeros((rows, n), BF)
        return jnp.concatenate(
            [
                pick(which * chan, chan),
                pick(INNER + CONVDIM + which * heads.heads, heads.heads),
                zeros(WIDE - chan - heads.heads),
                pick(INNER + which * chan, chan),
                zeros(WIDE - chan),
                w[:, 2 * INNER : 2 * INNER + 2 * STATE],
            ],
            axis=1,
        )

    other_rank = 4 * c_i + 2 * x_i + (1 - y_i)
    w_full = []
    for layer in range(layers):
        own = columns(layer, rank)
        got = swap(columns(layer, other_rank), "y", 1)
        pair = jnp.concatenate(
            [jnp.where(y_i == 0, own, got), jnp.where(y_i == 0, got, own)]
        )
        full = gather4(pair, ("zh", "zl"))
        w_full.append(full.reshape(width, COLS))

    extra = jnp.pad(gated_gain, ((0, 0), (0, width - chan)))[:, None, :]
    extra = jnp.pad(extra, ((0, 0), (0, ROWS - 1), (0, 0)))
    wo_pack = to_plane(jnp.concatenate([out_weight, extra], axis=1))
    gains = wo_pack[:, chan, :chan].astype(F32)
    w_out = [
        jnp.pad(wo_pack[layer, :chan], ((0, WIDE - chan), (0, 0))) for layer in range(layers)
    ]

    convs, params = [], []
    for layer in range(layers):
        taps = [lay(layer * CONV + k, per) for k in range(CONV)]
        full = jnp.stack(taps + [lay(layers * CONV + layer, per)])
        part = jnp.concatenate(
            [
                lax.dynamic_slice_in_dim(full, rank * chan, chan, 1),
                jnp.zeros((CONV + 1, WIDE - chan), F32),
                full[:, INNER:],
            ],
            axis=1,
        )
        convs.append(jnp.pad(part, ((0, 8 - CONV - 1), (0, 0))))
        per_head = lambda v: jnp.pad(
            lax.dynamic_slice_in_dim(v[layer], rank * heads.heads, heads.heads, 0),
            (heads.base, WIDE - heads.base - heads.heads),
        )
        skip = jnp.repeat(
            lax.dynamic_slice_in_dim(d_skip[layer], rank * heads.heads, heads.heads, 0), heads.p
        )
        wide = lambda v: jnp.pad(v, (0, WIDE - chan))
        params.append(
            jnp.pad(
                jnp.stack([per_head(dt_bias), per_head(a_log), wide(skip), wide(gains[layer])]),
                ((0, 4), (0, 0)),
            )
        )

    u0 = to_plane(u_mine)
    cot = to_plane(out_cotangent[0])
    gb1 = gather_plane(cot.astype(BF))

    length = group * span
    saves = [
        ((length, WIDE), F32),
        ((length + 8, 2 * WIDE), F32),
        ((length, WIDE), F32),
        ((group, STATE, WIDE), F32),
    ]
    scratch = [pltpu.VMEM((length + 16, LANES), F32), pltpu.VMEM((STATE, WIDE), F32)]
    back_scratch = [
        pltpu.VMEM((length + 16, LANES), F32),
        pltpu.VMEM((length + 8, 2 * WIDE), F32),
        pltpu.VMEM((STATE, WIDE), F32),
    ]

    def forward(layer, h, gb=None):
        out_rows = span if gb is not None else span + ROWS
        outs = [((group, out_rows, width), BF), ((group, 8, LANES), F32)] + saves
        args = (h, w_full[layer], w_out[layer], convs[layer], params[layer], seg)
        if gb is not None:
            args = args + (gb,)
        return call(
            partial(forward_kernel, heads, group, span, gb is not None), outs, scratch, *args
        )

    def backward(layer, gb, rq, saved):
        outs = [
            ((length, COLS), BF),
            ((group, span, width), BF),
            ((length, WIDE), BF),
            ((ROWS, 2 * WIDE), F32),
        ]
        return call(
            partial(backward_kernel, heads, group, span),
            outs,
            back_scratch,
            gb,
            w_full[layer],
            w_out[layer],
            convs[layer],
            params[layer],
            seg,
            rq,
            *saved,
        )

    got0 = forward(0, hx)
    sums0 = scatter_plane(got0[0])
    pre0 = sums0[:span]
    r0 = lax.rsqrt(sums0[span, :span] / INNER + EPS)
    u1 = u0 + pre0 * r0[:, None]
    h1 = gather_plane(rms(u1, n_gain[1]).astype(BF))

    got1 = forward(1, h1, gb1)
    stats = sum_plane(got1[1])
    r1 = lax.rsqrt(stats[:, 0] / INNER + EPS)
    q1 = r1 * r1 * r1 * stats[:, 1] / INNER
    rq1 = jnp.pad(jnp.stack([r1, q1], axis=1), ((0, 0), (0, 6), (0, 0)))

    def through_norm(d_h, u, gain):
        s = lax.rsqrt(jnp.mean(u * u, axis=-1, keepdims=True) + EPS)
        d_n = d_h * gain
        inner = jnp.mean(u * d_n, axis=-1, keepdims=True)
        return s * d_n - u * (s * s * s) * inner

    dproj1, dh1, yn1, sm1 = backward(1, gb1, rq1, got1[2:])
    grad = cot + through_norm(scatter_plane(dh1), u1, n_gain[1])
    gb = grad.astype(BF)
    s0 = jnp.sum(gb.astype(F32) * pre0, axis=-1)
    q0 = r0 * r0 * r0 * s0 / INNER
    tail = jnp.stack(split16(r0) + split16(q0))
    tail = jnp.pad(tail, ((0, ROWS - 4), (0, width - span)))
    gb0 = gather_plane(jnp.concatenate([gb, tail]))
    tails = gb0[:, span : span + 4, :span].astype(F32)
    rq0 = jnp.stack([tails[:, 0] + tails[:, 1], tails[:, 2] + tails[:, 3]], axis=1)
    rq0 = jnp.pad(rq0, ((0, 0), (0, 6), (0, 0)))

    dproj0, dh0, yn0, sm0 = backward(0, gb0, rq0, got0[2:])
    grad = grad + through_norm(scatter_plane(dh0), u0, n_gain[0])
    grad_input = to_plane(grad)

    own_r1 = lax.dynamic_index_in_dim(r1, rank, 0, False)
    output = to_plane(u1 + scatter_plane(got1[0]) * own_r1[:, None])

    def reduce_layer(layer, h, dproj, gb_all, yn, sm):
        g_in = tn(h[:, :span].reshape(length, width), dproj)
        g_out = tn(yn, gb_all[:, :span].reshape(length, width))[:chan]
        sm = jnp.pad(sm, ((0, 0), (0, COLS - sm.shape[1])))
        chunks = jnp.concatenate(
            [
                g_in.reshape(4, width // 4, COLS),
                g_out.reshape(4, chan // 4, width),
                jnp.broadcast_to(sm[None], (4,) + sm.shape),
            ],
            axis=1,
        ).astype(BF)
        total = lax.dynamic_index_in_dim(chunks, z_i, 0, False).astype(F32)
        for k in (1, 2, 3):
            part = lax.dynamic_index_in_dim(chunks, z_i ^ k, 0, False)
            total = total + swap(part, ("zh", "zl"), k).astype(F32)
        total = total.astype(BF)
        g_rows = total[: 2 * rows].reshape(2, rows, COLS)
        quarter = to_plane(total[2 * rows : 2 * rows + chan // 4])
        sm = total[2 * rows + chan // 4 :]
        keep = lax.dynamic_index_in_dim(g_rows, y_i, 0, False)
        send = lax.dynamic_index_in_dim(g_rows, 1 - y_i, 0, False)
        got = swap(jnp.concatenate([send, sm]), "y", 1)
        mine = jnp.concatenate([keep, sm])
        pair = jnp.concatenate(
            [jnp.where(y_i == 0, mine, got), jnp.where(y_i == 0, got, mine), quarter]
        )
        everyone = gather4(pair, ("x", "c"), (0, 2, 1, 3))
        g_owned = everyone[:, 2 * (rows + ROWS) :].reshape(chan, width).astype(F32)
        ranks = everyone[:, : 2 * (rows + ROWS)].reshape(group, rows + ROWS, COLS).astype(F32)
        return ranks, g_owned

    grads = [None] * layers
    for layer, h, dproj, gb_all, yn, sm in (
        (1, h1, dproj1, gb1, yn1, sm1),
        (0, hx, dproj0, gb0, yn0, sm0),
    ):
        ranks, g_owned = reduce_layer(layer, h, dproj, gb_all, yn, sm)
        g = ranks[:, :rows]
        flat = lambda v: jnp.moveaxis(v, 0, 1).reshape(v.shape[1], -1)
        bc = jnp.sum(g[:, :, 2 * WIDE :], axis=0)
        raw = jnp.concatenate(
            [
                flat(g[:, :, :chan]),
                flat(g[:, :, WIDE : WIDE + chan]),
                bc,
                flat(g[:, :, chan : chan + heads.heads]),
            ],
            axis=1,
        )
        g_ng = jnp.sum(raw * in_weight[layer].astype(F32), axis=1) / norm_gain[layer].astype(F32)
        sm = ranks[:, rows:]
        taps_all = jnp.concatenate(
            [flat(sm[:, : CONV + 1, :chan]), jnp.sum(sm[:, : CONV + 1, WIDE : 2 * WIDE], axis=0)],
            axis=1,
        )
        shard = 2 * z_i + y_i
        taps_own = lax.dynamic_slice_in_dim(taps_all, shard * per, per, 1)
        g_gg = lax.dynamic_index_in_dim(sm[:, 5, :chan], shard, 0, False)
        g_dsk = jnp.sum(sm[:, 6, :chan].reshape(HEADS, heads.p), axis=1)
        g_alog = sm[:, 7, heads.base : heads.base + heads.heads].reshape(HEADS)
        g_dtb = sm[:, 8, heads.base : heads.base + heads.heads].reshape(HEADS)
        grads[layer] = (
            raw, taps_own[:CONV], taps_own[CONV], g_alog, g_dtb, g_dsk, g_ng, g_gg, g_owned
        )
    stacked = [jnp.stack([grads[layer][i] for layer in range(layers)]) for i in range(9)]
    return (output[None], grad_input[None], *stacked)


def plane_fits(mesh, in_weight_rows=None):
    return mesh.shape["rep"] == 4 and mesh.shape["shard"] == 8


def solution(mesh):
    if plane_fits(mesh):
        fine = Mesh(mesh.devices.reshape(2, 2, 2, 2, 2), AXES)
        return sharded(plane_device, fine, ("x", "c"), ("zh", "zl", "y"))
    return sharded(per_device, mesh, "rep", "shard")


def sharded(function, mesh, rep, shard):
    return jax.shard_map(
        function,
        mesh=mesh,
        in_specs=(
            P(rep, shard, None),
            P(rep, shard),
            P(None, shard, None),
            P(None, None, shard),
            P(None, shard),
            P(),
            P(),
            P(),
            P(None, shard),
            P(None, shard),
            P(None, shard, None),
            P(rep, shard, None),
        ),
        out_specs=(
            P(rep, shard, None),
            P(rep, shard, None),
            P(None, shard, None),
            P(None, None, shard),
            P(None, shard),
            P(),
            P(),
            P(),
            P(None, shard),
            P(None, shard),
            P(None, shard, None),
        ),
        check_vma=False,
    )
```

```python
from functools import partial

import jax
import jax.numpy as jnp
from jax import lax
from jax.experimental import pallas as pl
from jax.experimental.pallas import tpu as pltpu
from jax.sharding import Mesh
from jax.sharding import PartitionSpec as P


HEADS = 24
STATE = 128
HEADDIM = 64
CONV = 4
SPAN = 128
INNER = 1536
CONVDIM = 1792


EPS = 1e-05
HIGH = lax.Precision.HIGHEST


def passed_along(x, axis, by):
    count = lax.axis_size(axis)
    pairs = [(i, i + by) for i in range(count) if 0 <= i + by < count]
    return lax.ppermute(x, axis, pairs)


def carried_in(part, axis, combine, identity, reverse):
    count = lax.axis_size(axis)
    place = lax.axis_index(axis)
    ahead = count - 1 - place if reverse else place
    gathered = jax.tree.map(lambda a: lax.all_gather(a, axis), part)
    state = jax.tree.map(lambda a, e: jnp.zeros_like(a) + jnp.asarray(e, a.dtype), part, identity)

    def one(turn, state):
        source = count - 1 - turn if reverse else turn
        return combine(
            state, jax.tree.map(lambda a: lax.dynamic_index_in_dim(a, source, 0, False), gathered)
        )

    return lax.fori_loop(0, ahead, one, state)


def rms(values, gain):
    return values * lax.rsqrt(jnp.mean(values * values, axis=-1, keepdims=True) + EPS) * gain


def span_step(carry, pieces):
    state, last = carry
    xs, bs, cs, dts, das, segs = pieces
    width = segs.shape[0]
    cum = jnp.cumsum(das, axis=0)
    rows = lax.broadcasted_iota(jnp.int32, (width, width), 0)
    cols = lax.broadcasted_iota(jnp.int32, (width, width), 1)
    mask = ((rows >= cols) & (segs[:, None] == segs[None, :])).astype(jnp.float32)
    cum_t = cum.T
    diff = cum_t[:, :, None] - cum_t[:, None, :]
    lmat = jnp.exp(jnp.where(mask[None] > 0, diff, 0.0)) * mask[None]
    scores = jnp.dot(cs, bs.T, precision=HIGH)
    mixing = lmat * scores[None] * dts.T[:, None, :]
    inside = jnp.einsum("hij,jhp->ihp", mixing, xs, precision=HIGH)
    valid = (segs == last).astype(jnp.float32)
    carried = jnp.einsum("in,hnp->ihp", cs, state, precision=HIGH)
    carried = carried * (jnp.exp(cum) * valid[:, None])[:, :, None]
    tail = (segs == segs[-1]).astype(jnp.float32)
    decay = jnp.exp(cum[-1][None, :] - cum) * tail[:, None] * dts
    keep = jnp.exp(cum[-1]) * (segs[-1] == last).astype(jnp.float32)
    fresh = jnp.einsum("jh,jn,jhp->hnp", decay, bs, xs, precision=HIGH)
    return ((state * keep[:, None, None] + fresh, segs[-1]), inside + carried)


def front(xbc, rim, dt_raw, conv_w, conv_b, dtb, alog, keeps):
    length = xbc.shape[0]
    padded = jnp.concatenate([rim, xbc], 0)
    total = conv_b
    for k in range(CONV):
        total = total + conv_w[k] * padded[k : k + length] * keeps[k][:, None]
    conv_out = jax.nn.silu(total)
    xs = conv_out[:, :INNER].reshape(length, HEADS, HEADDIM)
    bs = conv_out[:, INNER : INNER + STATE]
    cs = conv_out[:, INNER + STATE :]
    dts = jax.nn.softplus(dt_raw + dtb)
    return (xs, bs, cs, dts, -dts * jnp.exp(alog))


def local_states(xs, bs, cs, dts, das, seg, seg_prev):
    length = seg.shape[0]
    count = length // SPAN
    pieces = (
        xs.reshape(count, SPAN, HEADS, HEADDIM),
        bs.reshape(count, SPAN, STATE),
        cs.reshape(count, SPAN, STATE),
        dts.reshape(count, SPAN, HEADS),
        das.reshape(count, SPAN, HEADS),
        seg.reshape(count, SPAN),
    )
    start = (jnp.zeros((HEADS, STATE, HEADDIM), jnp.float32), seg[0])
    (final, _), ys = lax.scan(span_step, start, pieces)
    passing = jnp.exp(jnp.sum(das, axis=0)) * (seg[-1] == seg_prev).astype(jnp.float32)
    return (ys.reshape(length, HEADS, HEADDIM), passing, final)


def finish(z_part, xs, cs, das, y_local, entering, dskip, ggain, seg, seg_prev):
    length = seg.shape[0]
    cum = jnp.cumsum(das, axis=0)
    valid = (seg == seg_prev).astype(jnp.float32)
    from_before = jnp.einsum("tn,hnp->thp", cs, entering, precision=HIGH)
    from_before = from_before * (jnp.exp(cum) * valid[:, None])[:, :, None]
    ys = y_local + from_before + dskip[None, :, None] * xs
    gated = ys.reshape(length, INNER) * jax.nn.silu(z_part)
    return rms(gated, ggain)


def combine(earlier, later):
    return (earlier[0] * later[0], later[0][:, None, None] * earlier[1] + later[1])


def gather_layer(in_weight, out_weight, conv_weight, conv_bias, norm_gain, gated_gain, layer):
    return (
        lax.all_gather(in_weight[layer], "shard", axis=0, tiled=True),
        lax.all_gather(out_weight[layer], "shard", axis=0, tiled=True),
        lax.all_gather(conv_weight[layer], "shard", axis=1, tiled=True),
        lax.all_gather(conv_bias[layer], "shard", axis=0, tiled=True),
        lax.all_gather(norm_gain[layer], "shard", axis=0, tiled=True),
        lax.all_gather(gated_gain[layer], "shard", axis=0, tiled=True),
    )


def per_device(
    residual,
    segment_ids,
    in_weight,
    conv_weight,
    conv_bias,
    a_log,
    dt_bias,
    d_skip,
    norm_gain,
    gated_gain,
    out_weight,
    out_cotangent,
):
    u_now = residual[0]
    seg = segment_ids[0]
    length = seg.shape[0]
    layers = in_weight.shape[0]
    rim_ids = passed_along(seg[length - CONV + 1 :], "shard", 1)
    seg_ext = jnp.concatenate([rim_ids, seg])
    seg_prev = rim_ids[CONV - 2]
    keeps = jnp.stack([(seg_ext[k : k + length] == seg).astype(jnp.float32) for k in range(CONV)])
    identity = (jnp.ones((HEADS,), jnp.float32), jnp.zeros((HEADS, STATE, HEADDIM), jnp.float32))
    saved = []
    for layer in range(layers):
        weights = gather_layer(
            in_weight, out_weight, conv_weight, conv_bias, norm_gain, gated_gain, layer
        )
        w_in, w_out, conv_w, conv_b, n_gain, g_gain = weights
        normed, norm_pull = jax.vjp(rms, u_now, n_gain.astype(jnp.float32))
        hidden = normed.astype(jnp.bfloat16)
        proj = jnp.dot(hidden, w_in, preferred_element_type=jnp.float32)
        z_part = proj[:, :INNER]
        xbc = proj[:, INNER : INNER + CONVDIM]
        dt_raw = proj[:, INNER + CONVDIM :]
        rim = passed_along(xbc[length - CONV + 1 :], "shard", 1)
        feats, front_pull = jax.vjp(
            partial(front, keeps=keeps),
            xbc,
            rim,
            dt_raw,
            conv_w.astype(jnp.float32),
            conv_b.astype(jnp.float32),
            dt_bias[layer],
            a_log[layer],
        )
        xs, bs, cs, dts, das = feats
        (y_local, passing, final), local_pull = jax.vjp(
            partial(local_states, seg=seg, seg_prev=seg_prev), xs, bs, cs, dts, das
        )
        entering = carried_in((passing, final), "shard", combine, identity, False)[1]
        yn, finish_pull = jax.vjp(
            partial(finish, seg=seg, seg_prev=seg_prev),
            z_part,
            xs,
            cs,
            das,
            y_local,
            entering,
            d_skip[layer],
            g_gain.astype(jnp.float32),
        )
        yn_b = yn.astype(jnp.bfloat16)
        u_now = u_now + jnp.dot(yn_b, w_out, preferred_element_type=jnp.float32)
        kept = None
        saved.append(
            (hidden, norm_pull, front_pull, local_pull, finish_pull, passing, entering, yn_b, kept)
        )
    grad = out_cotangent[0]
    owned = [None] * layers
    heads = [None] * layers
    for layer in reversed(range(layers)):
        hidden, norm_pull, front_pull, local_pull, finish_pull, passing, entering, yn_b, kept = (
            saved[layer]
        )
        weights = gather_layer(
            in_weight, out_weight, conv_weight, conv_bias, norm_gain, gated_gain, layer
        )
        w_in, w_out = (weights[0], weights[1])
        grad_b = grad.astype(jnp.bfloat16)
        g_out = jnp.dot(yn_b.T, grad_b, preferred_element_type=jnp.float32)
        d_yn = jnp.dot(grad_b, w_out.T, preferred_element_type=jnp.float32)
        d_z, d_xs1, d_cs1, d_das1, d_local, d_enter, g_dsk, g_gg = finish_pull(d_yn)
        later = carried_in((passing, d_enter), "shard", combine, identity, True)[1]
        d_passing = jnp.sum(later * entering, axis=(1, 2))
        d_xs2, d_bs, d_cs2, d_dts, d_das2 = local_pull((d_local, d_passing, later))
        d_xbc, d_rim, d_dtr, g_cw, g_cb, g_dtb, g_alog = front_pull(
            (d_xs1 + d_xs2, d_bs, d_cs1 + d_cs2, d_dts, d_das1 + d_das2)
        )
        back_rim = passed_along(d_rim, "shard", -1)
        d_xbc = d_xbc.at[length - CONV + 1 :].add(back_rim)
        d_proj = jnp.concatenate([d_z, d_xbc, d_dtr], 1).astype(jnp.bfloat16)
        g_in = jnp.dot(hidden.T, d_proj, preferred_element_type=jnp.float32)
        d_h = jnp.dot(d_proj, w_in.T, preferred_element_type=jnp.float32)
        d_u, g_ng = norm_pull(d_h)
        grad = grad + d_u
        shares = (
            lax.psum_scatter(g_in, "shard", scatter_dimension=0, tiled=True),
            lax.psum_scatter(g_out, "shard", scatter_dimension=0, tiled=True),
            lax.psum_scatter(g_cw, "shard", scatter_dimension=1, tiled=True),
            lax.psum_scatter(g_cb, "shard", scatter_dimension=0, tiled=True),
            lax.psum_scatter(g_ng, "shard", scatter_dimension=0, tiled=True),
            lax.psum_scatter(g_gg, "shard", scatter_dimension=0, tiled=True),
        )
        shares = lax.psum((shares[0], shares[1], shares[2], shares[3], shares[4], shares[5]), "rep")
        owned[layer] = shares
        heads[layer] = jnp.stack([g_alog, g_dtb, g_dsk])
    grads_in = jnp.stack([owned[k][0] for k in range(layers)])
    grads_out = jnp.stack([owned[k][1] for k in range(layers)])
    grads_cw = jnp.stack([owned[k][2] for k in range(layers)])
    grads_cb = jnp.stack([owned[k][3] for k in range(layers)])
    grads_ng = jnp.stack([owned[k][4] for k in range(layers)])
    grads_gg = jnp.stack([owned[k][5] for k in range(layers)])
    head_sums = lax.psum(jnp.stack(heads), ("rep", "shard"))
    return (
        u_now[None],
        grad[None],
        grads_in,
        grads_cw,
        grads_cb,
        head_sums[:, 0],
        head_sums[:, 1],
        head_sums[:, 2],
        grads_ng,
        grads_gg,
        grads_out,
    )


AXES = ("x", "c", "zh", "zl", "y")
LANES = 128
ROWS = 16
WIDE = 2 * LANES
COLS = 6 * LANES
FORWARD_WORK = 20 * 10**9
BACKWARD_WORK = 26 * 10**9
VMEM_LIMIT = 56 * 1024 * 1024
BF = jnp.bfloat16
F32 = jnp.float32


def nn(a, b, precision=None):
    return lax.dot_general(
        a, b, (((1,), (0,)), ((), ())), precision=precision, preferred_element_type=F32
    )


def nt(a, b, precision=None):
    return lax.dot_general(
        a, b, (((1,), (1,)), ((), ())), precision=precision, preferred_element_type=F32
    )


def tn(a, b, precision=None):
    return lax.dot_general(
        a, b, (((0,), (0,)), ((), ())), precision=precision, preferred_element_type=F32
    )


def sigmoid(v):
    return 1.0 / (1.0 + jnp.exp(-v))


def softplus(v):
    return jnp.maximum(v, 0.0) + jnp.log1p(jnp.exp(-jnp.abs(v)))


def iota(shape, axis):
    return lax.broadcasted_iota(jnp.int32, shape, axis)


class Heads:
    def __init__(self, heads, p):
        self.heads = heads
        self.p = p
        self.base = heads * p - LANES

    def spread(self, v):
        lane = iota((v.shape[0], WIDE), 1)
        out = jnp.zeros((v.shape[0], WIDE), F32)
        for h in range(self.heads):
            col = v[:, self.base + h : self.base + h + 1]
            inside = (lane >= h * self.p) & (lane < (h + 1) * self.p)
            out = jnp.where(inside, col, out)
        return out

    def gather_matrix(self):
        row = iota((WIDE, LANES), 0)
        lane = iota((WIDE, LANES), 1)
        hit = jnp.zeros((WIDE, LANES), F32)
        for h in range(self.heads):
            inside = (row >= h * self.p) & (row < (h + 1) * self.p) & (lane == self.base + h)
            hit = jnp.where(inside, 1.0, hit)
        return hit

    def gather(self, v):
        return nn(v, self.gather_matrix(), HIGH)

    def masked(self, v):
        lane = iota(v.shape, 1)
        return [
            jnp.where((lane >= h * self.p) & (lane < (h + 1) * self.p), v, 0.0)
            for h in range(self.heads)
        ]

    def valid(self, rows):
        lane = iota((rows, LANES), 1)
        return (lane >= self.base) & (lane < self.base + self.heads)


def column(row, span):
    return jnp.transpose(jnp.broadcast_to(row, (span, row.shape[1])))


def fill_ids(seg_ref, ids, count, span):
    ids[...] = jnp.full(ids.shape, -1.0, F32)

    def one(k, _):
        row = seg_ref[k][0:1, :]
        ids[pl.ds(pl.multiple_of(8 + k * span, 8), span), :] = column(row, span)
        return 0

    lax.fori_loop(0, count, one, 0)


def times4(mask):
    return jnp.concatenate([mask] * 4, axis=1)


def taps_in(xpad, ids, start, cols, cw, span):
    near = xpad[pl.ds(start, span + 8), :]
    near_ids = ids[pl.ds(start, span + 8), :]
    total = cw[4:5, :] + cw[3:4, :] * near[8:]
    kept = []
    for k in range(3):
        same = times4((near_ids[5 + k : 5 + k + span] == cols).astype(F32))
        kept.append(near[5 + k : 5 + k + span] * same)
        total = total + cw[k : k + 1, :] * kept[k]
    kept.append(near[8:])
    return total, kept


def span_terms(heads, zdt, hp, seg_ref, k, span):
    row = seg_ref[k][0:1, :]
    before = seg_ref[jnp.maximum(k - 1, 0)][0:1, span - 1 : span]
    last = row[:, span - 1 : span]
    cols = column(row, span)
    raw = zdt[:, LANES:] + hp[0:1, :LANES]
    ok = heads.valid(span)
    dts = jnp.where(ok, softplus(raw), 0.0)
    rate = jnp.exp(hp[1:2, :LANES])
    das = -dts * rate
    ri, ci = iota((span, span), 0), iota((span, span), 1)
    tri = (ri >= ci).astype(F32)
    cum = nn(tri, das, HIGH)
    mask = (ri >= ci) & (cols == row)
    total = cum[span - 1 : span, :]
    enter = jnp.exp(cum) * (cols == before).astype(F32)
    leave = jnp.exp(total - cum) * (cols == last).astype(F32)
    keep = jnp.exp(total) * (last == before).astype(F32)
    cum_t = jnp.transpose(cum)
    decays = []
    for h in range(heads.heads):
        at = heads.base + h
        diff = cum[:, at : at + 1] - cum_t[at : at + 1, :]
        decays.append(jnp.where(mask, jnp.exp(jnp.where(mask, diff, 0.0)), 0.0))
    return raw, dts, rate, das, enter, leave, keep, decays, cols


def place(me_ref, k):
    return (k // 4) ^ me_ref[0], (k % 4) ^ me_ref[1]


def take(me_ref, pair, k, at, size):
    half, entry = place(me_ref, k)
    near, far = (ref[entry, pl.ds(at, size), :] for ref in pair)
    return jnp.where(half == 0, near, far)


def put(me_ref, pair, k, at, size, value):
    half, entry = place(me_ref, k)
    for side, ref in enumerate(pair):

        @pl.when(half == side)
        def _():
            ref[entry, pl.ds(at, size), :] = value


def fill_out_weight(wo_ref, wo, chan):
    wo[...] = jnp.zeros_like(wo)
    wo[pl.ds(0, chan + ROWS), :] = wo_ref[pl.ds(0, chan + ROWS), :]
    return wo_ref[pl.ds(chan, ROWS), :][0:1, :WIDE].astype(F32)


def forward_kernel(heads, count, span, with_back, *refs):
    me_ref = refs[0]
    h_ref = refs[1:3]
    w_ref, packed_ref, cw_ref, hp_ref = refs[3:7]
    if with_back:
        seg_ref, gb_ref = refs[7], refs[8:10]
        out_ref = refs[10:12]
        stat_ref, zdt_ref, xbc_ref, y_ref, s_ref, ids, wo_ref, state = refs[12:]
    else:
        out_ref = refs[7:9]
        seg_ref, zdt_ref, xbc_ref, y_ref, s_ref, ids, wo_ref, state = refs[9:]

        def unpack(k, _):
            seg_ref[k] = take(me_ref, h_ref, k, span, ROWS)[:8, :LANES].astype(F32)
            return 0

        lax.fori_loop(0, count, unpack, 0)
    fill_ids(seg_ref, ids, count, span)
    gain = fill_out_weight(packed_ref, wo_ref, heads.heads * heads.p)
    state[...] = jnp.zeros_like(state)
    xbc_ref[pl.ds(0, 8), :] = jnp.zeros((8, xbc_ref.shape[1]), F32)
    cw = cw_ref[...]
    hp = hp_ref[...]

    def one(k, _):
        start = pl.multiple_of(k * span, span)
        proj = nn(take(me_ref, h_ref, k, 0, span), w_ref[...])
        zdt = proj[:, :WIDE]
        zdt_ref[pl.ds(start, span), :] = zdt
        xbc_ref[pl.ds(start + 8, span), :] = proj[:, WIDE:]
        _, dts, _, _, enter, leave, keep, decays, cols = span_terms(
            heads, zdt, hp, seg_ref, k, span
        )
        pre, _ = taps_in(xbc_ref, ids, start, cols, cw, span)
        xc = pre * sigmoid(pre)
        x = xc[:, :WIDE]
        b16 = xc[:, WIDE : WIDE + LANES].astype(BF)
        c16 = xc[:, WIDE + LANES :].astype(BF)
        scores = nt(c16, b16)
        mixing = jnp.concatenate([(d * scores).astype(BF) for d in decays], axis=1)
        xdt = x * heads.spread(dts)
        stacked = jnp.concatenate([v.astype(BF) for v in heads.masked(xdt)], axis=0)
        y = nn(mixing, stacked)
        s_now = state[...]
        s_ref[k] = s_now
        y = y + nn(c16, s_now.astype(BF)) * heads.spread(enter)
        y = y + x * hp[2:3, :]
        fresh = tn(b16, (x * heads.spread(leave * dts)).astype(BF))
        state[...] = s_now * heads.spread(keep) + fresh
        y_ref[pl.ds(start, span), :] = y
        z = zdt
        gated = y * (z * sigmoid(z))
        ones = jnp.ones((8, WIDE), F32)
        squares = nt(ones, gated * gated, HIGH)
        scaled = gated * gain
        put(me_ref, out_ref, k, 0, span, nn(scaled.astype(BF), wo_ref[...]).astype(BF))
        if with_back:
            d_yn = nt(take(me_ref, gb_ref, k, 0, span), wo_ref[...])
            dots = nt(ones, scaled * d_yn, HIGH)
            pick = iota((8, LANES), 0) == 0
            stat_ref[k] = jnp.where(pick, squares, dots)
        else:
            tail = jnp.concatenate([squares, squares], axis=0)
            rest = jnp.zeros((ROWS, COLS - LANES), F32)
            tail = jnp.concatenate([tail, rest], axis=1).astype(BF)
            put(me_ref, out_ref, k, span, ROWS, tail)
        return 0

    lax.fori_loop(0, count, one, 0)


def backward_kernel(heads, count, span, tails, *refs):
    me_ref = refs[0]
    gb_ref = refs[1:3]
    w_ref, packed_ref, cw_ref, hp_ref, seg_ref = refs[3:8]
    if tails:
        refs = refs[8:]
    else:
        rq_ref = refs[8]
        refs = refs[9:]
    zdt_ref, xbc_ref, y_ref, s_ref = refs[:4]
    dproj_ref = refs[4]
    dh_ref = refs[5:7]
    yn_ref, sm_ref, ids, wo_ref, dpad, d_state = refs[7:]
    fill_ids(seg_ref, ids, count, span)
    gain = fill_out_weight(packed_ref, wo_ref, heads.heads * heads.p)
    d_state[...] = jnp.zeros_like(d_state)
    sm_ref[...] = jnp.zeros_like(sm_ref)
    length = count * span
    dpad[pl.ds(length, 8), :] = jnp.zeros((8, dpad.shape[1]), F32)
    cw = cw_ref[...]
    hp = hp_ref[...]

    def add(row, value):
        sm_ref[row : row + 1, : value.shape[1]] += value

    def one(turn, _):
        k = count - 1 - turn
        start = pl.multiple_of(k * span, span)
        zdt = zdt_ref[pl.ds(start, span), :]
        raw, dts, rate, das, enter, leave, keep, decays, cols = span_terms(
            heads, zdt, hp, seg_ref, k, span
        )
        pre, kept = taps_in(xbc_ref, ids, start, cols, cw, span)
        sp = sigmoid(pre)
        xc = pre * sp
        x = xc[:, :WIDE]
        b16 = xc[:, WIDE : WIDE + LANES].astype(BF)
        c16 = xc[:, WIDE + LANES :].astype(BF)
        y = y_ref[pl.ds(start, span), :]
        z = zdt
        sz = sigmoid(z)
        silu = z * sz
        gated = y * silu
        if tails:
            rows = take(me_ref, gb_ref, k, span, ROWS)[:8, :LANES].astype(F32)
            rq = jnp.concatenate([rows[0:1] + rows[1:2], rows[2:3] + rows[3:4]], axis=0)
        else:
            rq = rq_ref[k]
        half, entry = place(me_ref, k)
        r = jnp.concatenate([column(rq[0:1, :], span)] * 2, axis=1)
        q = jnp.concatenate([column(rq[1:2, :], span)] * 2, axis=1)
        normed = gated * r
        yn_ref[half, entry] = (normed * gain).astype(BF)
        d_yn = nt(take(me_ref, gb_ref, k, 0, span), wo_ref[...])
        add(5, jnp.sum(normed * d_yn, axis=0, keepdims=True))
        d_gated = r * gain * d_yn - gated * q
        dy = d_gated * silu
        dz = d_gated * y * (sz * (1.0 + z * (1.0 - sz)))
        add(6, jnp.sum(dy * x, axis=0, keepdims=True))
        dx = hp[2:3, :] * dy
        s_now = s_ref[k]
        s16 = s_now.astype(BF)
        dy_in = dy * heads.spread(enter)
        dy_in16 = dy_in.astype(BF)
        from_state = nn(c16, s16)
        d_cum = heads.gather(dy_in * from_state)
        dc = nt(dy_in16, s16)
        ds_next = d_state[...]
        ds16 = ds_next.astype(BF)
        wide_leave = heads.spread(leave * dts)
        b_ds = nn(b16, ds16)
        dx = dx + b_ds * wide_leave
        db = nt((x * wide_leave).astype(BF), ds16)
        d_leave = heads.gather(x * b_ds)
        through = d_leave * leave * dts
        held = jnp.sum(ds_next * s_now, axis=0, keepdims=True)
        held = heads.gather(jnp.broadcast_to(held, (8, WIDE)))[0:1, :] * keep
        d_state[...] = ds_next * heads.spread(keep) + tn(c16, dy_in16)
        scores = nt(c16, b16)
        wide_dt = heads.spread(dts)
        xdt = x * wide_dt
        dys = jnp.concatenate([v.astype(BF) for v in heads.masked(dy)], axis=0)
        d_mix = nt(dys, xdt.astype(BF))
        d_scores = jnp.zeros((span, span), F32)
        mixings = []
        lane = iota((span, LANES), 1)
        line = iota((LANES, span), 0)
        firsts = jnp.zeros((span, LANES), F32)
        seconds = jnp.zeros((LANES, span), F32)
        for h in range(heads.heads):
            dm = d_mix[h * span : (h + 1) * span, :] * decays[h]
            d_scores = d_scores + dm
            mixings.append((decays[h] * scores).astype(BF))
            flow = dm * scores
            at = heads.base + h
            firsts = jnp.where(lane == at, jnp.sum(flow, axis=1, keepdims=True), firsts)
            seconds = jnp.where(line == at, jnp.sum(flow, axis=0, keepdims=True), seconds)
        d_cum = d_cum + firsts - jnp.transpose(seconds) - through
        d_xdt = tn(jnp.concatenate(mixings, axis=0), dys)
        ds_16 = d_scores.astype(BF)
        dc = dc + nn(ds_16, b16)
        db = db + tn(ds_16, c16)
        dx = dx + d_xdt * wide_dt
        d_dt = heads.gather(x * d_xdt) + d_leave * leave
        at_end = held + jnp.sum(through, axis=0, keepdims=True)
        ri, ci = iota((span, span), 0), iota((span, span), 1)
        d_das = nn((ri <= ci).astype(F32), d_cum, HIGH) + at_end
        d_dt = d_dt - d_das * rate
        add(7, jnp.sum(d_das * das, axis=0, keepdims=True))
        d_raw = jnp.where(heads.valid(span), d_dt * sigmoid(raw), 0.0)
        add(8, jnp.sum(d_raw, axis=0, keepdims=True))
        dzdt = dz + jnp.concatenate([jnp.zeros((span, LANES), F32), d_raw], axis=1)
        d_pre = jnp.concatenate([dx, db, dc], axis=1) * (sp * (1.0 + pre * (1.0 - sp)))
        dpad[pl.ds(start, span), :] = d_pre
        add(4, jnp.sum(d_pre, axis=0, keepdims=True))
        for t in range(4):
            add(t, jnp.sum(d_pre * kept[t], axis=0, keepdims=True))
        d_xbc = cw[3:4, :] * d_pre
        near = dpad[pl.ds(start, span + 8), :]
        near_ids = ids[pl.ds(start + 8, span + 8), :]
        for t in range(3):
            ahead = 3 - t
            same = times4((near_ids[ahead : ahead + span] == cols).astype(F32))
            d_xbc = d_xbc + cw[t : t + 1, :] * near[ahead : ahead + span] * same
        d_proj = jnp.concatenate([dzdt, d_xbc], axis=1).astype(BF)
        dproj_ref[half, entry] = d_proj
        put(me_ref, dh_ref, k, 0, span, nt(d_proj, w_ref[...]).astype(BF))
        return 0

    lax.fori_loop(0, count, one, 0)


def call(kernel, outs, scratch, work, me, *args):
    whole = pl.BlockSpec(memory_space=pltpu.VMEM)
    return pl.pallas_call(
        kernel,
        out_shape=[jax.ShapeDtypeStruct(s, d) for s, d in outs],
        in_specs=[pl.BlockSpec(memory_space=pltpu.SMEM)] + [whole] * len(args),
        out_specs=[whole] * len(outs),
        scratch_shapes=scratch,
        cost_estimate=pl.CostEstimate(flops=work, transcendentals=0, bytes_accessed=1 << 20),
        compiler_params=pltpu.CompilerParams(vmem_limit_bytes=VMEM_LIMIT),
    )(me, *args)


def after(first, *later):
    held = lax.optimization_barrier((first,) + later)[1:]
    return held[0] if len(held) == 1 else held


def swap(x, axes, by):
    count = lax.axis_size(axes)
    return lax.ppermute(x, axes, [(i, i ^ by) for i in range(count)])


def to_plane(x):
    pairs = []
    for i in range(16):
        xx, cc, zh, zl = (i >> 3) & 1, (i >> 2) & 1, (i >> 1) & 1, i & 1
        pairs.append((i, (zl << 3) | (zh << 2) | (cc << 1) | xx))
    return lax.ppermute(x, ("x", "c", "zh", "zl"), pairs)


def in_order(parts, me):
    stacked = jnp.stack(parts)
    return jnp.concatenate(
        [lax.dynamic_index_in_dim(stacked, me ^ j, 0, True) for j in range(len(parts))]
    )


def parts4(x, axes):
    return [x] + [swap(x, axes, k) for k in (1, 2, 3)]


def gather4(x, axes):
    return in_order(parts4(x, axes), lax.axis_index(axes))


def gather_plane(x):
    near = jnp.stack(parts4(x, ("x", "y")))
    return near, swap(near, "c", 1)


def halve_plane(near, far):
    return (near.astype(F32) + swap(far, "c", 1).astype(F32)).astype(BF)


def quarter_plane(half):
    total = half[0].astype(F32)
    for k in (1, 2, 3):
        total = total + swap(half[k], ("x", "y"), k).astype(F32)
    return total


def sum_plane(x):
    total = x
    for k in (1, 2, 3):
        total = total + swap(x, ("x", "y"), k)
    return total + swap(total, "c", 1)


def split16(v):
    high = v.astype(BF)
    return high, (v - high.astype(F32)).astype(BF)


def plane_device(
    residual,
    segment_ids,
    in_weight,
    conv_weight,
    conv_bias,
    a_log,
    dt_bias,
    d_skip,
    norm_gain,
    gated_gain,
    out_weight,
    out_cotangent,
):
    span = residual.shape[1]
    width = residual.shape[2]
    layers = in_weight.shape[0]
    rows = in_weight.shape[1]
    group = 8
    heads = Heads(HEADS // group, HEADDIM)
    chan = heads.heads * heads.p
    x_i, c_i, y_i = lax.axis_index("x"), lax.axis_index("c"), lax.axis_index("y")
    z_i = lax.axis_index(("zh", "zl"))
    rank = 4 * c_i + 2 * x_i + y_i

    per = conv_bias.shape[1]
    narrow = lambda v: jnp.pad(v, ((0, 0), (0, WIDE - v.shape[1])))
    small = jnp.concatenate(
        [narrow(conv_weight.reshape(layers * CONV, per)), narrow(conv_bias), narrow(norm_gain)]
    )
    small = jnp.pad(small, ((0, -small.shape[0] % ROWS), (0, 0)))
    pair = swap(small, "y", 1)
    pair = jnp.stack([jnp.where(y_i == 0, small, pair), jnp.where(y_i == 0, pair, small)])
    small = gather4(pair, ("zh", "zl")).reshape((group,) + small.shape).astype(F32)
    lay = lambda at, size: small[:, at, :size].reshape(-1)
    n_gain = [lay(layers * (CONV + 1) + layer, rows) for layer in range(layers)]

    def columns(layer, which):
        w = in_weight[layer]
        pick = lambda at, size: lax.dynamic_slice_in_dim(w, at, size, 1)
        zeros = lambda n: jnp.zeros((rows, n), BF)
        return jnp.concatenate(
            [
                pick(which * chan, chan),
                pick(INNER + CONVDIM + which * heads.heads, heads.heads),
                zeros(WIDE - chan - heads.heads),
                pick(INNER + which * chan, chan),
                zeros(WIDE - chan),
                w[:, 2 * INNER : 2 * INNER + 2 * STATE],
            ],
            axis=1,
        )

    other_rank = 4 * c_i + 2 * x_i + (1 - y_i)
    every = range(layers)
    got = swap(jnp.stack([columns(layer, other_rank) for layer in every]), "y", 1)
    pairs = []
    for layer in every:
        own, other = columns(layer, rank), got[layer]
        pairs.append(
            jnp.concatenate([jnp.where(y_i == 0, own, other), jnp.where(y_i == 0, other, own)])
        )
    whole_rows = lambda pair: gather4(pair, ("zh", "zl")).reshape(width, COLS)
    gain_row = jnp.pad(gated_gain[:, None, :], ((0, 0), (0, ROWS - 1), (0, width - chan)))
    wo_send = jnp.concatenate([out_weight, gain_row], axis=1)
    w_full = [whole_rows(pairs[0])]

    ids_row = jnp.broadcast_to(segment_ids[0].astype(F32)[None, :], (8, span))
    ids_row = jnp.pad(ids_row, ((0, 0), (0, width - span)))
    first = to_plane(jnp.concatenate([residual[0], ids_row]))
    u0 = first[:span]
    cot_high, cot_low = split16(out_cotangent[0])
    early = after(pairs[0], jnp.concatenate([wo_send[0], cot_high]))
    early = to_plane(early)
    ids_rows = jnp.concatenate([first[span:], first[span:]]).astype(BF)
    first = jnp.concatenate([rms(u0, n_gain[0]).astype(BF), ids_rows])
    hx = gather_plane(first)
    cot_high = early[chan + ROWS :]
    pair1, late = after(hx[0], pairs[1], jnp.concatenate([wo_send[1], cot_low]))
    rows1 = parts4(pair1, ("zh", "zl"))
    late = to_plane(late)
    cot_near = parts4(cot_high, ("x", "y"))
    me = jnp.stack([c_i, 2 * x_i + y_i]).astype(jnp.int32)

    convs, params = [], []
    for layer in range(layers):
        taps = [lay(layer * CONV + k, per) for k in range(CONV)]
        full = jnp.stack(taps + [lay(layers * CONV + layer, per)])
        part = jnp.concatenate(
            [
                lax.dynamic_slice_in_dim(full, rank * chan, chan, 1),
                jnp.zeros((CONV + 1, WIDE - chan), F32),
                full[:, INNER:],
            ],
            axis=1,
        )
        convs.append(jnp.pad(part, ((0, 8 - CONV - 1), (0, 0))))
        per_head = lambda v: jnp.pad(
            lax.dynamic_slice_in_dim(v[layer], rank * heads.heads, heads.heads, 0),
            (heads.base, WIDE - heads.base - heads.heads),
        )
        skip = jnp.repeat(
            lax.dynamic_slice_in_dim(d_skip[layer], rank * heads.heads, heads.heads, 0), heads.p
        )
        wide = lambda v: jnp.pad(v, (0, WIDE - chan))
        params.append(
            jnp.pad(
                jnp.stack([per_head(dt_bias), per_head(a_log), wide(skip)]),
                ((0, 5), (0, 0)),
            )
        )

    length = group * span
    saves = [
        ((length, WIDE), F32),
        ((length + 8, 2 * WIDE), F32),
        ((length, WIDE), F32),
        ((group, STATE, WIDE), F32),
    ]
    scratch = [
        pltpu.VMEM((length + 16, LANES), F32),
        pltpu.VMEM((WIDE, width), BF),
        pltpu.VMEM((STATE, WIDE), F32),
    ]
    back_scratch = [
        pltpu.VMEM((length + 16, LANES), F32),
        pltpu.VMEM((WIDE, width), BF),
        pltpu.VMEM((length + 8, 2 * WIDE), F32),
        pltpu.VMEM((STATE, WIDE), F32),
    ]

    def forward(layer, h, gb=None):
        if gb is None:
            out = ((4, span + ROWS, width), BF)
            args = ()
        else:
            out = ((4, span, width), BF)
            args = (seg,) + gb
        outs = [out, out, ((group, 8, LANES), F32)] + saves
        kernel = partial(forward_kernel, heads, group, span, gb is not None)
        fixed = (w_full[layer], w_out[layer], convs[layer], params[layer])
        return call(kernel, outs, scratch, FORWARD_WORK, me, *h, *fixed, *args)

    def backward(layer, gb, rq, saved):
        outs = [
            ((2, 4, span, COLS), BF),
            ((4, span, width), BF),
            ((4, span, width), BF),
            ((2, 4, span, WIDE), BF),
            ((ROWS, 2 * WIDE), F32),
        ]
        kernel = partial(backward_kernel, heads, group, span, rq is None)
        fixed = (w_full[layer], w_out[layer], convs[layer], params[layer], seg)
        if rq is not None:
            fixed = fixed + (rq,)
        return call(kernel, outs, back_scratch, BACKWARD_WORK, me, *gb, *fixed, *saved)

    def chunks_of(h, dproj, gb_all, yn, sm):
        tokens = lambda pair: jnp.concatenate([p[:, :span] for p in pair]).reshape(length, width)
        g_in = tn(tokens(h), dproj.reshape(length, COLS))
        g_out = tn(yn.reshape(length, WIDE), tokens(gb_all))[:chan]
        sm = jnp.pad(sm, ((0, 0), (0, COLS - sm.shape[1])))
        return jnp.concatenate(
            [
                g_in.reshape(4, width // 4, COLS),
                g_out.reshape(4, chan // 4, width),
                jnp.broadcast_to(sm[None], (4,) + sm.shape),
            ],
            axis=1,
        ).astype(BF)

    def sum_planes(chunks):
        total = lax.dynamic_index_in_dim(chunks, z_i, 0, False).astype(F32)
        for k in (1, 2, 3):
            part = lax.dynamic_index_in_dim(chunks, z_i ^ k, 0, False)
            total = total + swap(part, ("zh", "zl"), k).astype(F32)
        return total.astype(BF)

    def spread_rows(total):
        g_rows = total[: 2 * rows].reshape(2, rows, COLS)
        sm = total[2 * rows + chan // 4 :]
        quarter = to_plane(total[2 * rows : 2 * rows + chan // 4])
        keep = jnp.concatenate([lax.dynamic_index_in_dim(g_rows, y_i, 0, False), sm])
        send = jnp.concatenate([lax.dynamic_index_in_dim(g_rows, 1 - y_i, 0, False), sm])
        near = [keep] + [swap((keep, send)[k % 2], ("x", "y"), k) for k in (1, 2, 3)]
        near = jnp.stack(near)
        quarters = [quarter] + [swap(quarter, ("x", "c"), k) for k in (1, 2, 3)]
        return near, swap(near, "c", 1), jnp.stack(quarters)

    w_out = [early]
    near, far, seg, *saved0 = forward(0, hx)
    late, *moved = after(seg, late, *rows1, *cot_near)
    w_full.append(in_order(moved[:4], z_i).reshape(width, COLS))
    w_out.append(late)
    cot_low = late[chan + ROWS :]
    cot_near = jnp.stack(moved[4:])
    gb1 = (cot_near, swap(cot_near, "c", 1))
    sums0 = quarter_plane(halve_plane(near, far))
    pre0 = sums0[:span]
    r0 = lax.rsqrt(sums0[span, :span] / INNER + EPS)
    u1 = u0 + pre0 * r0[:, None]
    h1 = gather_plane(rms(u1, n_gain[1]).astype(BF))

    near1, far1, stats, *saved1 = forward(1, h1, gb1)
    stats = sum_plane(stats)
    r1 = lax.rsqrt(stats[:, 0] / INNER + EPS)
    q1 = r1 * r1 * r1 * stats[:, 1] / INNER
    rq1 = jnp.pad(jnp.stack([r1, q1], axis=1), ((0, 0), (0, 6), (0, 0)))
    half1 = halve_plane(near1, far1)
    half1 = after(rq1, half1)
    pre1 = quarter_plane(half1)

    def through_norm(d_h, u, gain):
        s = lax.rsqrt(jnp.mean(u * u, axis=-1, keepdims=True) + EPS)
        d_n = d_h * gain
        inner = jnp.mean(u * d_n, axis=-1, keepdims=True)
        return s * d_n - u * (s * s * s) * inner

    dproj1, near, far, yn1, sm1 = backward(1, gb1, rq1, saved1)
    dh1 = quarter_plane(halve_plane(near, far))
    grad = cot_high.astype(F32) + cot_low.astype(F32) + through_norm(dh1, u1, n_gain[1])
    gb = grad.astype(BF)
    s0 = jnp.sum(gb.astype(F32) * pre0, axis=-1)
    q0 = r0 * r0 * r0 * s0 / INNER
    tail = jnp.stack(split16(r0) + split16(q0))
    tail = jnp.pad(tail, ((0, ROWS - 4), (0, width - span)))
    gb0 = gather_plane(jnp.concatenate([gb, tail]))

    own_r1 = lax.dynamic_index_in_dim(r1, rank, 0, False)
    output = u1 + pre1 * own_r1[:, None]
    chunks1 = chunks_of(h1, dproj1, gb1, yn1, sm1)
    chunks1, output = after(gb0[1], chunks1, output)
    output = to_plane(output)
    total1 = sum_planes(chunks1)

    dproj0, near, far, yn0, sm0 = backward(0, gb0, None, saved0)
    chunks0 = chunks_of(hx, dproj0, gb0, yn0, sm0)
    total0 = sum_planes(chunks0)
    half0 = halve_plane(near, far)
    dh0 = quarter_plane(half0)
    grad = grad + through_norm(dh0, u0, n_gain[0])
    grad_input = to_plane(grad)
    spread1 = spread_rows(after(dproj0, total1))
    spread0 = spread_rows(total0)

    shard = 2 * z_i + y_i
    me = jnp.stack([c_i, 2 * x_i + y_i, 2 * x_i + c_i, shard]).astype(jnp.int32)
    outs = [
        ((layers, rows, in_weight.shape[2]), F32),
        ((layers, CONV, per), F32),
        ((layers, per), F32),
        ((layers, HEADS), F32),
        ((layers, HEADS), F32),
        ((layers, HEADS), F32),
        ((layers, rows), F32),
        ((layers, chan), F32),
        ((layers, chan, width), F32),
    ]
    gain = norm_gain.astype(F32)[:, None, :]
    big_in, big_out = outs[0], outs[-1]
    grads_in, grads_out, small1 = owner_call(
        partial(owner_kernel, heads, 1, rows),
        [big_in, big_out, ((ROWS, CONVDIM), F32)],
        1,
        me,
        spread1 + (in_weight, gain),
    )
    grads_in, grads_out, *owned = owner_call(
        partial(owner_kernel, heads, 0, rows),
        [big_in, big_out] + outs[1:-1],
        0,
        me,
        spread0 + (in_weight, gain, small1),
        (grads_in, grads_out),
    )
    return (output[None], grad_input[None], grads_in, *owned, grads_out)


def owner_call(kernel, outs, layer, me, args, held=()):
    one = lambda shape: pl.BlockSpec((1,) + shape[1:], lambda _: (layer, 0, 0))
    full = lambda shape: pl.BlockSpec(shape, lambda _: (0,) * len(shape))
    in_specs = [pl.BlockSpec(memory_space=pltpu.SMEM)]
    for at, v in enumerate(args):
        in_specs.append(one(v.shape) if at in (3, 4) else full(v.shape))
    in_specs += [pl.BlockSpec(memory_space=pl.ANY)] * len(held)
    return pl.pallas_call(
        kernel,
        grid=(1,),
        out_shape=[jax.ShapeDtypeStruct(s, d) for s, d in outs],
        in_specs=in_specs,
        out_specs=[one(s) for s, _ in outs[:2]] + [full(s) for s, _ in outs[2:]],
        input_output_aliases={1 + len(args) + i: i for i in range(len(held))},
        cost_estimate=pl.CostEstimate(flops=5 * 10**9, transcendentals=0, bytes_accessed=1 << 20),
        compiler_params=pltpu.CompilerParams(vmem_limit_bytes=VMEM_LIMIT),
    )(me, *args, *held)


def owner_kernel(heads, layer, rows, *refs):
    me_ref, pair, quarters, w_ref, gain_ref = refs[0], refs[1:3], refs[3], refs[4], refs[5]
    if layer == 1:
        in_ref, out_ref, small_ref = refs[6:]
    else:
        other_ref = refs[6]
        in_ref, out_ref = refs[9:11]
        taps_ref, bias_ref, alog_ref, dtb_ref, skip_ref, ng_ref, gg_ref = refs[11:]
    chan = heads.heads * heads.p
    quarter = chan // 4
    parts = [take(me_ref, pair, b, 0, rows).astype(F32) for b in range(8)]
    smalls = [take(me_ref, pair, b, rows, ROWS).astype(F32) for b in range(8)]
    both = sum(p[:, 2 * WIDE :] for p in parts)
    full = jnp.concatenate(
        [p[:, :chan] for p in parts]
        + [p[:, WIDE : WIDE + chan] for p in parts]
        + [both]
        + [p[:, chan : chan + heads.heads] for p in parts],
        axis=1,
    )
    in_ref[0] = full
    ones = jnp.ones((8, full.shape[1]), F32)
    along = nt(ones, full * w_ref[0].astype(F32), HIGH)[0:1] / gain_ref[0]
    tails = sum(v[:, WIDE : 2 * WIDE] for v in smalls)
    mixed = jnp.concatenate([v[:, :chan] for v in smalls] + [tails], axis=1)
    for q in range(4):
        entry = (2 * (q % 2) + q // 2) ^ me_ref[2]
        out_ref[0, q * quarter : (q + 1) * quarter, :] = quarters[entry].astype(F32)
    if layer == 1:
        small_ref[...] = mixed
        small_ref[ROWS - 1 : ROWS, :rows] = along
        return
    per = bias_ref.shape[1]
    shard = me_ref[3]
    whose, head = iota((INNER, LANES), 0), iota((INNER, LANES), 1)
    of_head = (whose // heads.p == head).astype(F32)
    lane = (head // heads.heads) * chan + heads.base + head % heads.heads
    of_lane = ((whose == lane) & (head < HEADS)).astype(F32)
    other = other_ref[...]
    for at, small in ((0, mixed), (1, other)):
        inner = small[:, :INNER]
        own = pltpu.roll(small[:8], lax.rem(CONVDIM - shard * per, CONVDIM), 1)
        taps_ref[at] = own[:CONV, :per]
        at = slice(at, at + 1)
        bias_ref[at, :] = own[CONV : CONV + 1, :per]
        own = pltpu.roll(inner[:8], lax.rem(INNER - shard * chan, INNER), 1)
        gg_ref[at, :] = own[5:6, :chan]
        skip_ref[at, :] = nn(inner, of_head, HIGH)[6:7, :HEADS]
        per_head = nn(inner, of_lane, HIGH)
        alog_ref[at, :] = per_head[7:8, :HEADS]
        dtb_ref[at, :] = per_head[8:9, :HEADS]
    ng_ref[0:1, :] = along
    ng_ref[1:2, :] = other[ROWS - 1 : ROWS, :rows]


def plane_fits(mesh):
    return mesh.shape["rep"] == 4 and mesh.shape["shard"] == 8


def solution(mesh):
    if plane_fits(mesh):
        fine = Mesh(mesh.devices.reshape(2, 2, 2, 2, 2), AXES)

        step = sharded(plane_device, fine, ("x", "c"), ("zh", "zl", "y"))
        return step
    return sharded(per_device, mesh, "rep", "shard")


def sharded(function, mesh, rep, shard):
    return jax.shard_map(
        function,
        mesh=mesh,
        in_specs=(
            P(rep, shard, None),
            P(rep, shard),
            P(None, shard, None),
            P(None, None, shard),
            P(None, shard),
            P(),
            P(),
            P(),
            P(None, shard),
            P(None, shard),
            P(None, shard, None),
            P(rep, shard, None),
        ),
        out_specs=(
            P(rep, shard, None),
            P(rep, shard, None),
            P(None, shard, None),
            P(None, None, shard),
            P(None, shard),
            P(),
            P(),
            P(),
            P(None, shard),
            P(None, shard),
            P(None, shard, None),
        ),
        check_vma=False,
    )
```
